32 devices in a mesh: member: 4 (over z), band: 4 (over y, core), tensor: 2 (over x).
Axes of the slice: x: 2, y: 2, z: 4, core: 2. Of those that a mesh axis runs over, the one named last changes fastest.
Arguments:
- prior_grids: bfloat16 [4, 4, 32, 128, 192], P('member', None, 'band'), may hold values from -6 to 6
- w_qkv: bfloat16 [192, 3, 192], P(None, None, 'tensor'), may hold values from -0.4375 to 0.4375
- w_out: bfloat16 [192, 192], P('tensor'), may hold values from -0.4375 to 0.4375
- w_up: bfloat16 [192, 768], P(None, 'tensor'), may hold values from -0.4375 to 0.4375
- w_down: bfloat16 [768, 192], P('tensor'), may hold values from -0.21875 to 0.21875
- head_weight: bfloat16 [192, 160], replicated, may hold values from -0.4375 to 0.4375
- pos_bias: bfloat16 [6, 128, 128], P('tensor'), may hold values from -6 to 400
- zonal_offsets: int32 [4], P('member'), may hold values from 0 to 127
- obs_index: int32 [2, 32, 128, 16], P('tensor', 'band', 'member'), may hold values from 0 to 319
- obs_count: int32 [2, 32, 128], P('tensor', 'band', 'member'), may hold values from 8 to 16
- obs_value: float32 [2, 32, 128, 16], P('tensor', 'band', 'member'), may hold values from -6 to 6
- obs_weight: float32 [2, 32, 128, 16], P('tensor', 'band', 'member'), may hold values from 1 to 30
Outputs:
- analysis: float32 [4, 4, 32, 128, 160], P(None, 'tensor', 'band', 'member')
The draws below stay inside these ranges and needn't reach their ends.
All inputs are finite; a program needn't handle non-finite values.
Results may differ from the reference program's by a relative error of at most 0.025.
Values may be sent and summed in bfloat16 or wider, within the bound.
No kernel may reach another device: no remote copies, remote signals or barrier semaphores. Data moves between devices by JAX's collectives and lax.ppermute only.
A program may use at most 64 MiB of HBM per device.

```python
import math
import jax
import jax.numpy as jnp
from jax import lax

C = 192
HEADS = 6
FF = 768
PATCH_PREDICTED = 160
HEAD_DIM = 32
LEV = 4
LAT_DEV = 8
WLON = 8
VERTICAL_DEPTH = 2
WTOK = 128
ZONAL_CELLS = 128
NOBS = 16
NEWTON = 8
SAMPLE_COUNT = 4
MERIDIAN_CELLS = 32
LEVW = 2
NS = 320


def draw_pos_bias(key, part):
    key_base = jax.random.fold_in(key, 11)
    base = jnp.clip(jax.random.normal(key_base, (HEADS, WTOK, WTOK), jnp.float32), -6.0, 6.0)
    return base.astype(jnp.bfloat16)


def with_ends(values, stream_key, least, top_value):
    longest = values.shape.index(max(values.shape))
    spots = []
    for shift in (0, 1):
        where = [jax.random.randint(jax.random.fold_in(stream_key, axis), (), 0, length) for axis, length in enumerate(values.shape)]
        where[longest] = (where[longest] + shift) % values.shape[longest]
        spots.append(tuple(where))
    return values.at[spots[0]].set(least).at[spots[1]].set(top_value)


def levels(rng, extent, shards, least, top_value):
    loudness = 1.0
    for position, shards_of in shards:
        draws = jax.random.uniform(jax.random.fold_in(jax.random.fold_in(rng, 6), position), (shards_of,), jnp.float32, least / len(shards), top_value / len(shards))
        loudness = loudness * jnp.repeat(jnp.exp(draws), extent[position] // shards_of).reshape((-1,) + (1,) * (len(extent) - 1 - position))
    return loudness


def gaussian(key, shape, deviation, reach, cuts=(), kind=jnp.bfloat16):
    values = deviation * jax.random.normal(key, shape, jnp.float32)
    if cuts:
        values = values * levels(key, shape, cuts, -0.22, 0.18)
    return jnp.clip(values, -reach, reach).astype(kind)


def setup_inputs(seed: int = 0) -> dict:
    splits = jax.random.split(jax.random.key(seed), 13)
    return {
        "prior_grids": gaussian(splits[0], (SAMPLE_COUNT, LEV, MERIDIAN_CELLS, ZONAL_CELLS, C), 1.0, 6.0, ((0, 4), (2, 4))),
        "w_qkv": gaussian(splits[1], (C, 3, C), C ** -0.5, 0.4375, ((2, 2),)),
        "w_out": gaussian(splits[2], (C, C), C ** -0.5, 0.4375, ((0, 2),)),
        "w_up": gaussian(splits[3], (C, FF), C ** -0.5, 0.4375, ((1, 2),)),
        "w_down": gaussian(splits[4], (FF, C), FF ** -0.5, 0.21875, ((0, 2),)),
        "head_weight": gaussian(splits[5], (C, PATCH_PREDICTED), C ** -0.5, 0.4375),
        "pos_bias": draw_pos_bias(jax.random.fold_in(splits[12], 71), 0),
        "zonal_offsets": with_ends(jax.random.randint(splits[7], (SAMPLE_COUNT,), 0, ZONAL_CELLS), jax.random.fold_in(splits[7], 1), 0, ZONAL_CELLS - 1).astype(jnp.int32),
        "obs_index": with_ends(jax.random.randint(splits[8], (LEVW, MERIDIAN_CELLS, ZONAL_CELLS, NOBS), 0, NS), jax.random.fold_in(splits[8], 1), 0, NS - 1).astype(jnp.int32),
        "obs_count": with_ends(jax.random.randint(splits[9], (LEVW, MERIDIAN_CELLS, ZONAL_CELLS), NOBS // 2, NOBS + 1), jax.random.fold_in(splits[9], 1), NOBS // 2, NOBS).astype(jnp.int32),
        "obs_value": gaussian(splits[10], (LEVW, MERIDIAN_CELLS, ZONAL_CELLS, NOBS), 1.0, 6.0, ((0, 2), (1, 4), (2, 4)), jnp.float32),
        "obs_weight": jnp.clip(jnp.exp(math.log(30.0) - 3.4011974 * jax.random.uniform(splits[11], (LEVW, MERIDIAN_CELLS, ZONAL_CELLS, NOBS), jnp.float32) ** levels(splits[11], (LEVW, MERIDIAN_CELLS, ZONAL_CELLS, NOBS), ((0, 2), (1, 4), (2, 4)), -0.2, 0.2)), 1.0, 30.0),
    }


def normalize(tokens):
    values = tokens.astype(jnp.float32)
    center = values - lax.optimization_barrier(jnp.mean(values, axis=-1, keepdims=True))
    spread = lax.optimization_barrier(jnp.mean(center * center, axis=-1, keepdims=True))
    return (center * lax.rsqrt(spread + 1e-05)).astype(jnp.bfloat16)

def feed_forward(hidden_in, w_up, w_down):
    normed = normalize(hidden_in).astype(jnp.float32)
    raised = jnp.einsum('...c,cf->...f', normed, w_up.astype(jnp.float32))
    active = jax.nn.gelu(raised, approximate=False).astype(jnp.bfloat16)
    return jnp.einsum('...f,fc->...c', active.astype(jnp.float32), w_down.astype(jnp.float32))

def batch_product(left_mat, right_mat):
    return jnp.einsum('ijp,jkp->ikp', left_mat, right_mat, precision=lax.Precision.HIGHEST)

def transform(sample_fields, obs_index, obs_count, obs_value, obs_weight):
    member_list = sample_fields.shape[0]
    output_width = sample_fields.shape[3]
    patch_count = sample_fields.shape[2]
    ens_flat = sample_fields.transpose(0, 1, 3, 2).reshape(member_list, -1, patch_count)
    center = lax.optimization_barrier(jnp.mean(ens_flat, axis=0))
    spread = ens_flat - center[None]
    picked = jnp.broadcast_to(obs_index.T[None], (member_list,) + obs_index.T.shape)
    observed = jnp.take_along_axis(ens_flat, picked, axis=1)
    obs_mean = lax.optimization_barrier(jnp.mean(observed, axis=0))
    obs_spread = observed - obs_mean[None]
    slot_ids = jnp.arange(obs_index.shape[1], dtype=jnp.int32)[:, None]
    live_mask = (slot_ids < obs_count[None, :]).astype(jnp.float32)
    weighted = obs_spread * (obs_weight.T * live_mask)[None]
    innovation = obs_value.T - obs_mean
    identity = jnp.eye(member_list, dtype=jnp.float32)[:, :, None]
    matrix = (member_list - 1.0) * identity + jnp.einsum('ikp,jkp->ijp', weighted, obs_spread, precision=lax.Precision.HIGHEST)
    right_side = jnp.einsum('ikp,kp->ip', weighted, innovation, precision=lax.Precision.HIGHEST)
    trace_sum = lax.optimization_barrier(jnp.sum(matrix * identity, axis=(0, 1)))
    iterate = matrix / trace_sum
    inverse_root = jnp.broadcast_to(identity, matrix.shape)
    for sweep_idx in range(NEWTON):
        factor = 1.5 * identity - 0.5 * batch_product(inverse_root, iterate)
        iterate = batch_product(iterate, factor)
        inverse_root = batch_product(factor, inverse_root)
    analysis_cov = batch_product(inverse_root, inverse_root) / trace_sum
    mean_weight = jnp.einsum('ijp,jp->ip', analysis_cov, right_side, precision=lax.Precision.HIGHEST)
    weights = mean_weight[:, None, :] + math.sqrt(member_list - 1.0) * inverse_root * lax.rsqrt(trace_sum)
    updated = center[None] + jnp.einsum('inp,imp->mnp', spread, weights, precision=lax.Precision.HIGHEST)
    return updated.reshape(member_list, VERTICAL_DEPTH, output_width, patch_count).transpose(0, 1, 3, 2)

def run_member(member_state, offset, w_qkv, w_out, w_up, w_down, head_weight, pos_bias):
    half_rows = LAT_DEV // 2
    blocks = (MERIDIAN_CELLS + 2 * half_rows) // LAT_DEV
    lev_win = LEV // VERTICAL_DEPTH
    lon_win = ZONAL_CELLS // WLON
    padded = jnp.pad(member_state, ((0, 0), (half_rows, half_rows), (0, 0), (0, 0)))
    rolled = jnp.roll(padded, -offset, axis=2)
    normed = normalize(rolled)
    windows = normed.reshape(lev_win, VERTICAL_DEPTH, blocks, LAT_DEV, lon_win, WLON, C).transpose(0, 2, 4, 1, 3, 5, 6).reshape(-1, WTOK, C)
    window_count = windows.shape[0]
    packed = jnp.einsum('gpc,cte->gpte', windows.astype(jnp.float32), w_qkv.astype(jnp.float32)).astype(jnp.bfloat16)
    queries = packed[:, :, 0].reshape(window_count, WTOK, HEADS, HEAD_DIM).astype(jnp.float32)
    keys_in = packed[:, :, 1].reshape(window_count, WTOK, HEADS, HEAD_DIM).astype(jnp.float32)
    values_in = packed[:, :, 2].reshape(window_count, WTOK, HEADS, HEAD_DIM).astype(jnp.float32)
    scores = jnp.einsum('gqhd,gkhd->ghqk', queries, keys_in) * HEAD_DIM ** (-0.5)
    scores = scores + pos_bias.astype(jnp.float32)[None]
    lat_pos = jnp.arange(WTOK, dtype=jnp.int32) // WLON % LAT_DEV
    row_global = jnp.arange(blocks, dtype=jnp.int32)[:, None] * LAT_DEV + lat_pos[None, :]
    usable = (row_global >= half_rows) & (row_global < MERIDIAN_CELLS + half_rows)
    usable = jnp.broadcast_to(usable[None, :, None, :], (lev_win, blocks, lon_win, WTOK)).reshape(window_count, WTOK)
    scores = jnp.where(usable[:, None, None, :], scores, -1000000000.0)
    softmaxed = jax.nn.softmax(scores, axis=-1).astype(jnp.bfloat16)
    mixture = jnp.einsum('ghqk,gkhd->gqhd', softmaxed.astype(jnp.float32), values_in).astype(jnp.bfloat16)
    mixture = mixture.reshape(window_count, WTOK, C)
    projected = jnp.einsum('gqe,ec->gqc', mixture.astype(jnp.float32), w_out.astype(jnp.float32))
    restored = projected.reshape(lev_win, blocks, lon_win, VERTICAL_DEPTH, LAT_DEV, WLON, C).transpose(0, 3, 1, 4, 2, 5, 6)
    restored = restored.reshape(LEV, blocks * LAT_DEV, ZONAL_CELLS, C)
    restored = jnp.roll(restored, offset, axis=2)[:, half_rows:half_rows + MERIDIAN_CELLS]
    section_one = member_state.astype(jnp.float32) + restored
    second_section = (section_one + feed_forward(section_one, w_up, w_down)).astype(jnp.bfloat16)
    return jnp.einsum('fngu,uz->fngz', second_section.astype(jnp.float32), head_weight.astype(jnp.float32))

def reference(prior_grids, w_qkv, w_out, w_up, w_down, head_weight, pos_bias, zonal_offsets, obs_index, obs_count, obs_value, obs_weight):

    def predict_one_sample(sample_collection):
        return run_member(sample_collection[0], sample_collection[1], w_qkv, w_out, w_up, w_down, head_weight, pos_bias)
    predict_samples = lax.map(predict_one_sample, (prior_grids, zonal_offsets))
    vertical_couples = LEV // VERTICAL_DEPTH
    divided_pieces = predict_samples.reshape(SAMPLE_COUNT, vertical_couples, VERTICAL_DEPTH, MERIDIAN_CELLS, ZONAL_CELLS, PATCH_PREDICTED).transpose(1, 0, 2, 3, 4, 5)
    divided_pieces = divided_pieces.reshape(vertical_couples, SAMPLE_COUNT, VERTICAL_DEPTH, MERIDIAN_CELLS * ZONAL_CELLS, PATCH_PREDICTED)

    def analyse(sample_collection):
        return transform(sample_collection[0], sample_collection[1], sample_collection[2], sample_collection[3], sample_collection[4])
    result = lax.map(analyse, (divided_pieces, obs_index.reshape(vertical_couples, MERIDIAN_CELLS * ZONAL_CELLS, NOBS), obs_count.reshape(vertical_couples, MERIDIAN_CELLS * ZONAL_CELLS), obs_value.reshape(vertical_couples, MERIDIAN_CELLS * ZONAL_CELLS, NOBS), obs_weight.reshape(vertical_couples, MERIDIAN_CELLS * ZONAL_CELLS, NOBS)))
    result = result.reshape(vertical_couples, SAMPLE_COUNT, VERTICAL_DEPTH, MERIDIAN_CELLS, ZONAL_CELLS, PATCH_PREDICTED).transpose(1, 0, 2, 3, 4, 5)
    return result.reshape(SAMPLE_COUNT, LEV, MERIDIAN_CELLS, ZONAL_CELLS, PATCH_PREDICTED)
```

```python
import functools
import math

import jax
import jax.numpy as jnp
from jax import lax
from jax.experimental import pallas as pl
from jax.experimental.pallas import tpu as pltpu
from jax.sharding import PartitionSpec as P

WLON = 8
DEPTH = 2
NEWTON = 8
LANES = 128
GROUP = 4
LOG2E = 1.4426950408889634
F32 = jnp.float32
BF16 = jnp.bfloat16


def nn(a, b):
    return lax.dot_general(a, b, (((1,), (0,)), ((), ())), preferred_element_type=F32)


def nt(a, b):
    return lax.dot_general(a, b, (((1,), (1,)), ((), ())), preferred_element_type=F32)


def tn(a, b):
    return lax.dot_general(a, b, (((0,), (0,)), ((), ())), preferred_element_type=F32)


def eye(n):
    return (
        lax.broadcasted_iota(jnp.int32, (n, n), 0) == lax.broadcasted_iota(jnp.int32, (n, n), 1)
    ).astype(BF16)


def to_dense(x):
    half = x.shape[0] // 2
    return jnp.concatenate(
        [x[:, :LANES], jnp.concatenate([x[:half, LANES:], x[half:, LANES:]], axis=1)], axis=0
    )


def from_dense(d):
    rows = d.shape[0] * 2 // 3
    half = rows // 2
    part = LANES // 2
    high = jnp.concatenate([d[rows:, :part], d[rows:, part:]], axis=0)
    del half
    return jnp.concatenate([d[:rows], high], axis=1)


def pack_kernel(prior, qkv, w_out, w_up, w_down, bias, a_ref, b_ref, top_ref, bot_ref, rows, sem):
    levs, n_rows, _, _ = rows.shape
    start = lax.axis_index("tensor") * levs
    copy = pltpu.make_async_copy(prior.at[pl.ds(start, levs)], rows, sem)
    copy.start()
    e_loc = qkv.shape[2]
    ident = eye(e_loc)
    a_rows = []
    for i in range(3):
        a_rows.append(nt(ident, qkv[i]).astype(BF16))
    dense = to_dense(jnp.concatenate(a_rows, axis=0))
    n_a = dense.shape[0]
    a_ref[:n_a] = dense
    heads, wtok, _ = bias.shape
    for h in range(heads):
        a_ref[n_a + h * wtok : n_a + (h + 1) * wtok] = bias[h]
    o = to_dense(w_out[...])
    r0 = o.shape[0]
    b_ref[:r0] = o
    up = to_dense(nt(eye(w_up.shape[1]), w_up[...]).astype(BF16))
    r1 = r0 + up.shape[0]
    b_ref[r0:r1] = up
    down = nt(eye(w_down.shape[1]), w_down[...]).astype(BF16)
    feats = down.shape[0]
    for i in range(down.shape[1] // LANES):
        b_ref[r1 + i * feats : r1 + (i + 1) * feats] = down[:, i * LANES : (i + 1) * LANES]
    copy.wait()
    half = n_rows // 2
    for lev in range(levs):
        for r in range(half):
            top_ref[lev * half + r] = to_dense(rows[lev, r])
            bot_ref[lev * half + r] = to_dense(rows[lev, half + r])


def pack(member_grid, qkv, w_out, w_up, w_down, bias, levs):
    _, n_rows, cols, feats = member_grid.shape
    e_loc = qkv.shape[2]
    heads, wtok, _ = bias.shape
    ff = w_up.shape[1]
    dn = feats * 3 // 2 * 0 + feats * 2 // 3 * 0 + LANES
    a_rows = 3 * e_loc * 3 // 2 + heads * wtok
    b_rows = e_loc * 3 // 2 + ff * 3 // 2 + feats * (ff // LANES)
    halo = (levs * n_rows // 2, cols * 3 // 2, dn)
    vm = pl.BlockSpec(memory_space=pltpu.VMEM)
    return pl.pallas_call(
        pack_kernel,
        out_shape=(
            jax.ShapeDtypeStruct((a_rows, LANES), BF16),
            jax.ShapeDtypeStruct((b_rows, LANES), BF16),
            jax.ShapeDtypeStruct(halo, BF16),
            jax.ShapeDtypeStruct(halo, BF16),
        ),
        in_specs=[pl.BlockSpec(memory_space=pl.ANY)] + [vm] * 5,
        out_specs=[vm] * 4,
        scratch_shapes=[
            pltpu.VMEM((levs, n_rows, cols, feats), BF16),
            pltpu.SemaphoreType.DMA,
        ],
        name="pack",
    )(member_grid, qkv, w_out, w_up, w_down, bias)


def gelu(x):
    return 0.5 * x * (1.0 + lax.erf(x * math.sqrt(0.5)))


def forecast_kernel(*refs, side, parts, dests, e_loc, heads_loc, ff_loc):
    offs, prior, halo, hw = refs[:4]
    a_parts = refs[4 : 4 + parts]
    b_parts = refs[4 + parts : 4 + 2 * parts]
    refs = refs[4 + 2 * parts :]
    outs = refs[:dests]
    (own, nscr, xscr, wq, wk, wv, wot, wup, wdt, bias, perm, fscr, sem) = refs[dests:]
    levs, half, cols, feats = own.shape
    n_rows = 2 * half
    wtok = levs * n_rows * WLON
    qtok = levs * half * WLON
    heads = heads_loc * parts
    head_dim = e_loc // heads_loc
    width = hw.shape[1]
    q_row = half - half * side

    start = lax.axis_index("tensor") * levs
    copy = pltpu.make_async_copy(
        prior.at[pl.ds(start, levs), side * half : (side + 1) * half], own, sem
    )
    copy.start()
    off = offs[0]
    me = lax.axis_index("member")
    band = lax.axis_index("band")
    if side == 0:
        is_open = band > 0
    else:
        is_open = band < lax.axis_size("band") - 1
    penalty = jnp.where(is_open, 0.0, -1000000000.0).astype(F32)

    j = lax.broadcasted_iota(jnp.int32, (cols, cols), 0) + off
    j = jnp.where(j >= cols, j - cols, j)
    rollm = (j == lax.broadcasted_iota(jnp.int32, (cols, cols), 1)).astype(BF16)

    for p in range(parts):
        n_a = 3 * e_loc * 3 // 2
        qkv = from_dense(a_parts[p][:n_a])
        rows = slice(p * e_loc, (p + 1) * e_loc)
        wq[rows] = qkv[:e_loc]
        wk[rows] = qkv[e_loc : 2 * e_loc]
        wv[rows] = qkv[2 * e_loc :]
        r0 = e_loc * 3 // 2
        r1 = r0 + ff_loc * 3 // 2
        wup[p * ff_loc : (p + 1) * ff_loc] = from_dense(b_parts[p][r0:r1])
        for i in range(ff_loc // LANES):
            lo = p * ff_loc + i * LANES
            wdt[:, lo : lo + LANES] = b_parts[p][r1 + i * feats : r1 + (i + 1) * feats]
    w_out = jnp.concatenate([from_dense(b_parts[p][: e_loc * 3 // 2]) for p in range(parts)], axis=0)
    wot[...] = nt(eye(feats), w_out.astype(F32).T.astype(BF16).T).astype(BF16)

    span = half * WLON
    pieces = []
    for p in range(parts):
        n_a = 3 * e_loc * 3 // 2
        for h in range(heads_loc):
            for lev in range(levs):
                lo = n_a + h * wtok + lev * n_rows * WLON + q_row * WLON
                pieces.append(a_parts[p][lo : lo + span].astype(F32))
    bias_t = jnp.concatenate(pieces, axis=0).T * LOG2E
    lat = (lax.broadcasted_iota(jnp.int32, (wtok, 1), 0) // WLON) % n_rows
    closed = (lat < half) if side == 0 else (lat >= half)
    bias[...] = bias_t + jnp.where(closed, penalty, 0.0)

    cw = cols // dests
    patches = half * cw
    rj = lax.broadcasted_iota(jnp.int32, (half * cols, LANES), 0)
    row = rj // cols
    col = rj - row * cols + off
    col = jnp.where(col >= cols, col - cols, col)
    dest = col // cw
    target = (dest ^ me) * patches + row * cw + (col - dest * cw)
    lane = lax.broadcasted_iota(jnp.int32, (half * cols, LANES), 1)
    for b in range(dests * patches // LANES):
        perm[:, b * LANES : (b + 1) * LANES] = (target == lane + b * LANES).astype(BF16)

    ones = jnp.ones((feats, feats), BF16)

    def norm(x):
        c = x.astype(F32) - nn(x, ones) * (1.0 / feats)
        v = nn((c * c).astype(BF16), ones) * (1.0 / feats)
        return (c * lax.rsqrt(v + 1e-05)).astype(BF16)

    def halo_rows(lev, carry):
        for r in range(half):
            x = from_dense(halo[lev * half + r])
            key_row = r if side == 0 else half + r
            nscr[lev, key_row] = nn(rollm, norm(x))
        return carry

    def own_rows(lev, carry):
        for r in range(half):
            x = own[lev, r]
            key_row = half + r if side == 0 else r
            nscr[lev, key_row] = nn(rollm, norm(x))
            xscr[lev, r] = nn(rollm, x)
        return carry

    copy.wait()
    lax.fori_loop(0, levs, own_rows, 0)
    lax.fori_loop(0, levs, halo_rows, 0)

    lane_q = lax.broadcasted_iota(jnp.int32, (1, LANES), 1)
    first = lane_q < qtok
    fl = (((1,), (0,)), ((), ()))
    del fl
    e_all = heads * head_dim
    mrow = lax.broadcasted_iota(jnp.int32, (e_all, heads * qtok), 0) // head_dim
    mcol = lax.broadcasted_iota(jnp.int32, (e_all, heads * qtok), 1) // qtok
    own_head = mrow == mcol
    n_pairs = heads * qtok // LANES
    pair_rows = e_all // n_pairs
    ones_rows = jnp.ones((16, wtok), BF16)
    ident = eye(feats)
    q_scale = head_dim**-0.5 * LOG2E

    def group(g, carry):
        base = g * (GROUP * WLON)
        keys, queries, raw = [], [], []
        for w in range(GROUP):
            at = pl.multiple_of(base + w * WLON, WLON)
            keys.append(nscr[:, :, pl.ds(at, WLON), :].reshape(wtok, feats).astype(BF16))
            q = nscr[:, q_row : q_row + half, pl.ds(at, WLON), :].reshape(qtok, feats).astype(BF16)
            queries += [q] * (LANES // qtok)
            raw.append(xscr[:, :, pl.ds(at, WLON), :].reshape(qtok, feats).astype(BF16))
        x_all = jnp.concatenate(keys, axis=0)
        k_all = nt(x_all, wk[...]).astype(BF16)
        v_all = nt(wv[...], x_all).astype(BF16)
        q_all = (nt(wq[...], jnp.concatenate(queries, axis=0)) * q_scale).astype(BF16)
        mixed = []
        for w in range(GROUP):
            qt = q_all[:, w * LANES : (w + 1) * LANES]
            qm = jnp.where(own_head, jnp.concatenate([qt] * n_pairs, axis=1), jnp.zeros((), BF16))
            s = nn(k_all[w * wtok : (w + 1) * wtok], qm) + bias[...]
            p = jnp.exp2(s - jnp.max(s, axis=0, keepdims=True)).astype(BF16)
            vt = v_all[:, w * wtok : (w + 1) * wtok]
            pieces = []
            for jp in range(n_pairs):
                rows = jnp.concatenate([vt[jp * pair_rows : (jp + 1) * pair_rows], ones_rows], axis=0)
                o = nn(rows, p[:, jp * LANES : (jp + 1) * LANES])
                o = o[:pair_rows] / o[pair_rows : pair_rows + 1]
                turned = pltpu.roll(o, qtok, 1)
                mid = pair_rows // 2
                if w % 2 == 0:
                    pieces += [o[:mid], turned[mid:]]
                else:
                    pieces += [turned[:mid], o[mid:]]
            mixed.append(jnp.concatenate(pieces, axis=0))
        mix = jnp.concatenate(
            [jnp.where(first, mixed[i], mixed[i + 1]) for i in range(0, GROUP, 2)], axis=1
        ).astype(BF16)
        s1 = nn(wot[...], mix) + nt(ident, jnp.concatenate(raw, axis=0))
        c = s1 - jnp.mean(s1, axis=0, keepdims=True)
        v = jnp.mean(c * c, axis=0, keepdims=True)
        n2 = (c * lax.rsqrt(v + 1e-05)).astype(BF16)
        act = gelu(nn(wup[...], n2)).astype(BF16)
        s2 = (s1 + nn(wdt[...], act)).astype(BF16)
        f = tn(s2, hw[...])
        for w in range(GROUP):
            at = pl.multiple_of(base + w * WLON, WLON)
            fscr[:, :, pl.ds(at, WLON), :] = f[w * qtok : (w + 1) * qtok].reshape(
                levs, half, WLON, width
            )
        return carry

    lax.fori_loop(0, cols // (GROUP * WLON), group, 0)

    for lev in range(levs):
        f = fscr[lev].reshape(half * cols, width).astype(BF16)
        o = tn(f, perm[...]).astype(BF16)
        for d in range(dests):
            outs[d][lev] = o[:, d * patches : (d + 1) * patches]


def forecast(offs, member_grid, halo, hw, a_parts, b_parts, *, side, dests, levs, heads_loc):
    _, n_rows, cols, feats = member_grid.shape
    half = n_rows // 2
    parts = len(a_parts)
    head_dim = feats // (heads_loc * parts)
    e_loc = heads_loc * head_dim
    width = hw.shape[1]
    ff_loc = (b_parts[0].shape[0] - e_loc * 3 // 2) * 2 * LANES // (3 * LANES + 2 * feats)
    wtok = levs * n_rows * WLON
    qtok = levs * half * WLON
    heads = heads_loc * parts
    patches = half * (cols // dests)
    vm = pl.BlockSpec(memory_space=pltpu.VMEM)
    return pl.pallas_call(
        functools.partial(
            forecast_kernel,
            side=side,
            parts=parts,
            dests=dests,
            e_loc=e_loc,
            heads_loc=heads_loc,
            ff_loc=ff_loc,
        ),
        out_shape=[jax.ShapeDtypeStruct((levs, width, patches), BF16)] * dests,
        in_specs=[pl.BlockSpec(memory_space=pltpu.SMEM), pl.BlockSpec(memory_space=pl.ANY)]
        + [vm] * (2 + 2 * parts),
        out_specs=[vm] * dests,
        scratch_shapes=[
            pltpu.VMEM((levs, half, cols, feats), BF16),
            pltpu.VMEM((levs, n_rows, cols, feats), F32),
            pltpu.VMEM((levs, half, cols, feats), F32),
            pltpu.VMEM((feats, feats), BF16),
            pltpu.VMEM((feats, feats), BF16),
            pltpu.VMEM((feats, feats), BF16),
            pltpu.VMEM((feats, feats), BF16),
            pltpu.VMEM((ff_loc * parts, feats), BF16),
            pltpu.VMEM((feats, ff_loc * parts), BF16),
            pltpu.VMEM((wtok, heads * qtok), F32),
            pltpu.VMEM((half * cols, dests * patches), BF16),
            pltpu.VMEM((levs, half, cols, width), F32),
            pltpu.SemaphoreType.DMA,
        ],
        name=f"forecast_{side}",
    )(offs, member_grid, halo, hw, *a_parts, *b_parts)


def analysis_kernel(*refs, members, side):
    x_refs = refs[:members]
    idx, weight, value = refs[members : members + 3]
    out = refs[-1]
    levs, width, patches = x_refs[0].shape
    slots = idx.shape[1]
    half, cw = out.shape[2], out.shape[3]
    xs = [[x_refs[m][lev].astype(F32) for lev in range(levs)] for m in range(members)]
    state = lax.broadcasted_iota(jnp.int32, (width, patches), 0)
    pairs = [(i, k) for i in range(members) for k in range(i, members)]
    mat = {p: None for p in pairs}
    rhs = [None] * members
    for k in range(slots):
        at = idx[0, k : k + 1]
        hits = [state + lev * width == at for lev in range(levs)]
        y = []
        for m in range(members):
            total = jnp.where(hits[0], xs[m][0], 0.0)
            for lev in range(1, levs):
                total = jnp.where(hits[lev], xs[m][lev], total)
            y.append(jnp.sum(total, axis=0, keepdims=True))
        y_mean = sum(y[1:], y[0]) * (1.0 / members)
        yp = [v - y_mean for v in y]
        r = weight[0, k : k + 1]
        d = value[0, k : k + 1] - y_mean
        for i in range(members):
            ry = r * yp[i]
            for n in range(i, members):
                t = ry * yp[n]
                mat[i, n] = t if k == 0 else mat[i, n] + t
            t = ry * d
            rhs[i] = t if k == 0 else rhs[i] + t
    for i in range(members):
        mat[i, i] = mat[i, i] + (members - 1.0)
    trace = sum([mat[i, i] for i in range(1, members)], mat[0, 0])
    inv = 1.0 / trace

    def entry(a, i, n):
        return a[pairs.index((min(i, n), max(i, n)))]

    def times(a, b):
        res = []
        for i, n in pairs:
            acc = entry(a, i, 0) * entry(b, 0, n)
            for q in range(1, members):
                acc = acc + entry(a, i, q) * entry(b, q, n)
            res.append(acc)
        return res

    def sweep(_, carry):
        g, z = carry
        zg = times(z, g)
        f = [(1.5 if i == n else 0.0) - 0.5 * v for (i, n), v in zip(pairs, zg)]
        return times(g, f), times(f, z)

    g0 = [mat[p] * inv for p in pairs]
    z0 = [jnp.full_like(trace, 1.0 if i == n else 0.0) for i, n in pairs]
    _, z = lax.fori_loop(0, NEWTON, sweep, (g0, z0))
    zz = times(z, z)
    root = math.sqrt(members - 1.0) * lax.rsqrt(trace)
    mean_w = []
    for i in range(members):
        acc = entry(zz, i, 0) * rhs[0]
        for n in range(1, members):
            acc = acc + entry(zz, i, n) * rhs[n]
        mean_w.append(acc * inv)
    me = lax.axis_index("member")
    centers, spreads = [], []
    for lev in range(levs):
        total = xs[0][lev]
        for m in range(1, members):
            total = total + xs[m][lev]
        c = total * (1.0 / members)
        centers.append(c)
        spreads.append([xs[m][lev] - c for m in range(members)])
    for m in range(members):
        w = [mean_w[i] + root * entry(z, i, m) for i in range(members)]
        for lev in range(levs):
            acc = centers[lev]
            for i in range(members):
                acc = acc + spreads[lev][i] * w[i]
            out[m ^ me, lev] = acc.T.reshape(half, cw, width)


def analysis(xs, idx, weight, value, out_shape, side, prev):
    members = len(xs)
    levs, width, patches = xs[0].shape
    _, _, n_rows, cw, _ = out_shape
    half = n_rows // 2
    slots = idx.shape[1]
    vm = pl.BlockSpec(memory_space=pltpu.VMEM)
    obs = pl.BlockSpec((1, slots, patches), lambda i: (side, 0, 0))
    args = [*xs, idx, weight, value]
    specs = [pl.BlockSpec((levs, width, patches), lambda i: (0, 0, 0))] * members + [obs] * 3
    aliases = {}
    if prev is not None:
        aliases = {len(args): 0}
        args.append(prev)
        specs.append(pl.BlockSpec(memory_space=pl.ANY))
    del vm
    return pl.pallas_call(
        functools.partial(analysis_kernel, members=members, side=side),
        grid=(1,),
        out_shape=jax.ShapeDtypeStruct(out_shape, F32),
        in_specs=specs,
        out_specs=pl.BlockSpec((members, levs, half, cw, width), lambda i: (0, 0, side, 0, 0)),
        input_output_aliases=aliases,
        name=f"analysis_{side}",
    )(*args)


def from_others(array, axis):
    size = lax.axis_size(axis)
    return [array] + [
        lax.ppermute(array, axis, [(i, (i + s) % size) for i in range(size)])
        for s in range(1, size)
    ]


def shards(
    prior_grids,
    w_qkv,
    w_out,
    w_up,
    w_down,
    head_weight,
    pos_bias,
    zonal_offsets,
    obs_index,
    obs_count,
    obs_value,
    obs_weight,
):
    member_grid = prior_grids[0]
    levs = member_grid.shape[0] // lax.axis_size("tensor")
    n_rows = member_grid.shape[1]
    dests = lax.axis_size("member")
    bands = lax.axis_size("band")
    heads_loc = pos_bias.shape[0]

    a_mine, b_mine, top, bottom = pack(
        member_grid, w_qkv.transpose(1, 0, 2), w_out, w_up, w_down, pos_bias, levs
    )
    a_parts = from_others(a_mine, "tensor")
    up = [(i, i + 1) for i in range(bands - 1)]
    above = lax.ppermute(bottom, "band", up)
    below = lax.ppermute(top, "band", [(b, a) for a, b in up])
    b_parts = from_others(b_mine, "tensor")

    slots = obs_index.shape[-1]
    cw = obs_index.shape[2]
    patches = n_rows // 2 * cw

    def slots_first(a):
        return a.reshape(2, patches, slots).transpose(0, 2, 1)

    live = jnp.arange(slots, dtype=jnp.int32) < obs_count[..., None]
    idx = slots_first(obs_index)
    weight = slots_first(jnp.where(live, obs_weight, 0.0))
    value = slots_first(obs_value)

    received = []
    for side, halo in ((0, above), (1, below)):
        sent = forecast(
            zonal_offsets,
            member_grid,
            halo,
            head_weight,
            a_parts,
            b_parts,
            side=side,
            dests=dests,
            levs=levs,
            heads_loc=heads_loc,
        )
        received.append(
            [sent[0]]
            + [
                lax.ppermute(sent[k], "member", [(i, i ^ k) for i in range(dests)])
                for k in range(1, dests)
            ]
        )
    out_shape = (dests, levs, n_rows, cw, head_weight.shape[1])
    result = None
    for side in range(2):
        result = analysis(received[side], idx, weight, value, out_shape, side, result)
    return result


def solution(mesh):
    return jax.shard_map(
        shards,
        mesh=mesh,
        in_specs=(
            P("member", None, "band", None, None),
            P(None, None, "tensor"),
            P("tensor", None),
            P(None, "tensor"),
            P("tensor", None),
            P(),
            P("tensor", None, None),
            P("member"),
            P("tensor", "band", "member", None),
            P("tensor", "band", "member"),
            P("tensor", "band", "member", None),
            P("tensor", "band", "member", None),
        ),
        out_specs=P(None, "tensor", "band", "member", None),
        check_vma=False,
    )
```

```python
import functools
import math

import jax
import jax.numpy as jnp
from jax import lax
from jax.experimental import pallas as pl
from jax.experimental.pallas import tpu as pltpu
from jax.sharding import PartitionSpec as P


WLON = 8
NEWTON = 8
LANES = 128
GROUP = 4
LOG2E = 1.4426950408889634
F32 = jnp.float32
BF16 = jnp.bfloat16


VMEM = pltpu.VMEM
PARAMS = pltpu.CompilerParams(vmem_limit_bytes=32 * 1024 * 1024)


def near(x):
    return pltpu.with_memory_space_constraint(x, pltpu.VMEM)


def nn(a, b):
    return lax.dot_general(a, b, (((1,), (0,)), ((), ())), preferred_element_type=F32)


def nt(a, b):
    return lax.dot_general(a, b, (((1,), (1,)), ((), ())), preferred_element_type=F32)


def tn(a, b):
    return lax.dot_general(a, b, (((0,), (0,)), ((), ())), preferred_element_type=F32)


def eye(n):
    return (
        lax.broadcasted_iota(jnp.int32, (n, n), 0) == lax.broadcasted_iota(jnp.int32, (n, n), 1)
    ).astype(BF16)


def to_dense(x):
    half = x.shape[0] // 2
    return jnp.concatenate(
        [x[:, :LANES], jnp.concatenate([x[:half, LANES:], x[half:, LANES:]], axis=1)], axis=0
    )


def from_dense(d):
    rows = d.shape[0] * 2 // 3
    half = rows // 2
    part = LANES // 2
    high = jnp.concatenate([d[rows:, :part], d[rows:, part:]], axis=0)
    del half
    return jnp.concatenate([d[:rows], high], axis=1)


def pack_kernel(qkv, w_out, w_up, w_down, bias, a_ref, b_ref):
    ident = eye(qkv.shape[2])
    dense = to_dense(jnp.concatenate([nt(ident, qkv[i]).astype(BF16) for i in range(3)], axis=0))
    n_a = dense.shape[0]
    a_ref[:n_a] = dense
    heads, wtok, _ = bias.shape
    for h in range(heads):
        a_ref[n_a + h * wtok : n_a + (h + 1) * wtok] = bias[h]
    o = to_dense(w_out[...])
    r0 = o.shape[0]
    b_ref[:r0] = o
    up = to_dense(nt(eye(w_up.shape[1]), w_up[...]).astype(BF16))
    r1 = r0 + up.shape[0]
    b_ref[r0:r1] = up
    feats, ff = w_down.shape
    for i in range(ff // LANES):
        b_ref[r1 + i * feats : r1 + (i + 1) * feats] = w_down[:, i * LANES : (i + 1) * LANES]


def pack(qkv, w_out, w_up, w_down, bias):
    _, feats, e_loc = qkv.shape
    heads, wtok, _ = bias.shape
    ff = w_up.shape[1]
    a_rows = 3 * e_loc * 3 // 2 + heads * wtok
    b_rows = e_loc * 3 // 2 + ff * 3 // 2 + feats * (ff // LANES)
    vm = pl.BlockSpec(memory_space=pltpu.VMEM)
    return pl.pallas_call(
        pack_kernel,
        out_shape=(VMEM((a_rows, LANES), BF16), VMEM((b_rows, LANES), BF16)),
        in_specs=[vm] * 5,
        out_specs=[vm] * 2,
        compiler_params=PARAMS,
        name="pack",
    )(qkv, w_out, w_up, w_down, bias)


def prologue_kernel(offs, prior, above, below, hw_t, obs_i, obs_n, obs_v, obs_w, *refs):
    n_refs, raw_refs, hw, perm, idx, val, wgt, own, xscr, sem = refs[:2], refs[2:4], *refs[4:]
    levs, n_rows, feats, cols = own.shape
    half = n_rows // 2
    windows = cols // WLON
    start = lax.axis_index("tensor") * levs
    copy = pltpu.make_async_copy(prior.at[pl.ds(start, levs)], own, sem)
    copy.start()
    off = offs[0]
    me = lax.axis_index("member")
    dests = lax.axis_size("member")
    hw[...] = nt(eye(feats), hw_t[...]).astype(BF16)

    slot = lax.broadcasted_iota(jnp.int32, obs_i.shape[1:], 0)
    for side in range(2):
        at = range(side * half, (side + 1) * half)
        idx[side] = jnp.concatenate([obs_i[r] for r in at], axis=1)
        val[side] = jnp.concatenate([obs_v[r] for r in at], axis=1)
        wgt[side] = jnp.concatenate(
            [jnp.where(slot < obs_n[r : r + 1], obs_w[r], 0.0) for r in at], axis=1
        )

    j = lax.broadcasted_iota(jnp.int32, (cols, cols), 0) + off
    j = jnp.where(j >= cols, j - cols, j)
    rollm = (j == lax.broadcasted_iota(jnp.int32, (cols, cols), 1)).astype(BF16)

    cw = cols // dests
    patches = half * cw
    lane = lax.broadcasted_iota(jnp.int32, (cols, LANES), 1)
    col = lax.broadcasted_iota(jnp.int32, (cols, LANES), 0) + off
    col = jnp.where(col >= cols, col - cols, col)
    dest = col // cw
    base = (dest ^ me) * patches + (col - dest * cw)
    for r in range(half):
        for b in range(dests * patches // LANES):
            hit = base + r * cw == lane + b * LANES
            perm[r * cols : (r + 1) * cols, b * LANES : (b + 1) * LANES] = hit.astype(BF16)

    def norm(x):
        x = x.astype(F32)
        c = x - jnp.sum(x, axis=0, keepdims=True) * (1.0 / feats)
        v = jnp.sum(c * c, axis=0, keepdims=True) * (1.0 / feats)
        return (c * lax.rsqrt(v + 1e-05)).astype(BF16)

    def by_window(first, second):
        f = first.reshape(windows, 1, WLON, feats)
        s = second.reshape(windows, 1, WLON, feats)
        return jnp.concatenate([f, s], axis=1).reshape(windows, 2 * WLON, feats).astype(BF16)

    copy.wait()
    for side in range(2):
        halo = (above, below)[side]

        def one_level(lev, carry, side=side, halo=halo):
            for r in range(0, half, 2):
                x0, x1 = own[lev, side * half + r], own[lev, side * half + r + 1]
                own_row = half + r if side == 0 else r
                at = pl.multiple_of(lev * (n_rows * WLON) + own_row * WLON, 2 * WLON)
                n_refs[side][:, pl.ds(at, 2 * WLON), :] = by_window(
                    nt(rollm, norm(x0)), nt(rollm, norm(x1))
                )
                at = pl.multiple_of(lev * (half * WLON) + r * WLON, 2 * WLON)
                xscr[:, pl.ds(at, 2 * WLON), :] = by_window(nt(rollm, x0), nt(rollm, x1))
                h0, h1 = halo[lev, r], halo[lev, r + 1]
                halo_row = r if side == 0 else half + r
                at = pl.multiple_of(lev * (n_rows * WLON) + halo_row * WLON, 2 * WLON)
                n_refs[side][:, pl.ds(at, 2 * WLON), :] = by_window(
                    nt(rollm, norm(h0)), nt(rollm, norm(h1))
                )
            return carry

        lax.fori_loop(0, levs, one_level, 0)
        qtok = levs * half * WLON
        ident = eye(feats)
        for w in range(0, windows, GROUP):
            x = xscr[w : w + GROUP].reshape(GROUP * qtok, feats)
            raw_refs[side][:, w * qtok : (w + GROUP) * qtok] = nt(ident, x).astype(BF16)


def prologue(offs, prior_t, above, below, hw_t, obs, levs, dests):
    slots = obs[0].shape[1]
    patches = prior_t.shape[1] // 2 * (prior_t.shape[3] // dests)
    _, n_rows, feats, cols = prior_t.shape
    half = n_rows // 2
    windows = cols // WLON
    width = hw_t.shape[0]
    n_shape = VMEM((windows, levs * n_rows * WLON, feats), BF16)
    raw_shape = VMEM((feats, levs * half * cols), BF16)
    vm = pl.BlockSpec(memory_space=pltpu.VMEM)
    return pl.pallas_call(
        prologue_kernel,
        out_shape=(
            n_shape,
            n_shape,
            raw_shape,
            raw_shape,
            VMEM((feats, width), BF16),
            VMEM((half * cols, half * cols), BF16),
            VMEM((2, slots, patches), jnp.int32),
            VMEM((2, slots, patches), F32),
            VMEM((2, slots, patches), F32),
        ),
        in_specs=[pl.BlockSpec(memory_space=pltpu.SMEM), pl.BlockSpec(memory_space=pl.ANY)]
        + [vm] * 7,
        out_specs=[vm] * 9,
        scratch_shapes=[
            pltpu.VMEM((levs, n_rows, feats, cols), BF16),
            pltpu.VMEM((windows, levs * half * WLON, feats), BF16),
            pltpu.SemaphoreType.DMA,
        ],
        compiler_params=PARAMS,
        name="prologue",
    )(offs, prior_t, near(above), near(below), hw_t, *obs)


def gelu(x):
    return 0.5 * x * (1.0 + lax.erf(x * math.sqrt(0.5)))


def forecast_kernel(*refs, side, parts, dests, e_loc, heads_loc, ff_loc, levs, n_rows):
    n_ref, raw, hw, perm = refs[:4]
    a_parts = refs[4 : 4 + parts]
    b_parts = refs[4 + parts : 4 + 2 * parts]
    refs = refs[4 + 2 * parts :]
    outs = refs[:dests]
    (wq, wk, wv, wot, wup, wdt, bias, fscr) = refs[dests:]
    windows, wtok, feats = n_ref.shape
    half = n_rows // 2
    cols = windows * WLON
    qtok = levs * half * WLON
    heads = heads_loc * parts
    head_dim = e_loc // heads_loc
    width = hw.shape[1]
    q_row = half - half * side
    band = lax.axis_index("band")
    if side == 0:
        is_open = band > 0
    else:
        is_open = band < lax.axis_size("band") - 1
    penalty = jnp.where(is_open, 0.0, -1000000000.0).astype(F32)

    n_a = 3 * e_loc * 3 // 2
    r0 = e_loc * 3 // 2
    r1 = r0 + ff_loc * 3 // 2
    for p in range(parts):
        qkv = from_dense(a_parts[p][:n_a])
        rows = slice(p * e_loc, (p + 1) * e_loc)
        wq[rows] = qkv[:e_loc]
        wk[rows] = qkv[e_loc : 2 * e_loc]
        wv[rows] = qkv[2 * e_loc :]
        wup[p * ff_loc : (p + 1) * ff_loc] = from_dense(b_parts[p][r0:r1])
        for i in range(ff_loc // LANES):
            lo = p * ff_loc + i * LANES
            wdt[:, lo : lo + LANES] = b_parts[p][r1 + i * feats : r1 + (i + 1) * feats]
    w_out = jnp.concatenate([from_dense(b_parts[p][:r0]) for p in range(parts)], axis=0)
    wot[...] = tn(w_out, eye(heads * head_dim)).astype(BF16)

    span = half * WLON
    lat = (lax.broadcasted_iota(jnp.int32, (wtok, 1), 0) // WLON) % n_rows
    closed = (lat < half) if side == 0 else (lat >= half)
    shut = jnp.where(closed, penalty, 0.0)
    for p in range(parts):
        for h in range(heads_loc):
            rows = []
            for lev in range(levs):
                lo = n_a + h * wtok + lev * n_rows * WLON + q_row * WLON
                rows.append(a_parts[p][lo : lo + span].astype(F32))
            at = (p * heads_loc + h) * LANES
            bias[:, at : at + LANES] = (
                jnp.concatenate(rows * (LANES // qtok), axis=0).T * LOG2E + shut
            )

    first = lax.broadcasted_iota(jnp.int32, (1, LANES), 1) < qtok
    zero = jnp.zeros((), BF16)
    q_scale = head_dim**-0.5 * LOG2E
    e_all = heads * head_dim

    def zeros(rows):
        return jnp.zeros((rows, LANES), BF16)

    def attention(g):
        x = n_ref[g * GROUP : (g + 1) * GROUP]
        x_all = x.reshape(GROUP * wtok, feats)
        lo = q_row * WLON
        x_q = x.reshape(GROUP * levs, n_rows * WLON, feats)[:, lo : lo + span, :]
        k_all = nt(x_all, wk[...])
        v_all = nt(wv[...], x_all).astype(BF16)
        q_all = (nt(wq[...], x_q.reshape(GROUP * qtok, feats)) * q_scale).astype(BF16)
        mixed = []
        for pair in range(GROUP // 2):
            k0 = k_all[2 * pair * wtok : (2 * pair + 1) * wtok]
            k1 = k_all[(2 * pair + 1) * wtok : (2 * pair + 2) * wtok]
            q_t = q_all[:, pair * LANES : (pair + 1) * LANES]
            qa = jnp.where(first, q_t, zero)
            qb = jnp.where(first, zero, q_t)
            v_t = v_all[:, 2 * pair * wtok : (2 * pair + 2) * wtok]
            probs, inverse = [], []
            for e0 in range(0, e_all, LANES):
                dims = min(LANES, e_all - e0)
                if dims == LANES:
                    lhs = jnp.concatenate([k0[:, e0 : e0 + LANES], k1[:, e0 : e0 + LANES]], axis=1)
                else:
                    lhs = jnp.concatenate([k0[:, e0 : e0 + dims], k1[:, e0 : e0 + dims]], axis=1)
                columns = []
                for h in range(dims // head_dim):
                    a = e0 + h * head_dim
                    gaps = (h * head_dim, dims - (h + 1) * head_dim)
                    col = []
                    for q in (qa, qb):
                        if gaps[0]:
                            col.append(zeros(gaps[0]))
                        col.append(q[a : a + head_dim])
                        if gaps[1]:
                            col.append(zeros(gaps[1]))
                    columns.append(jnp.concatenate(col, axis=0))
                s = nn(lhs.astype(BF16), jnp.concatenate(columns, axis=1))
                for h in range(dims // head_dim):
                    at = (e0 // head_dim + h) * LANES
                    t = s[:, h * LANES : (h + 1) * LANES] + bias[:, at : at + LANES]
                    p = jnp.exp2(t - jnp.max(t, axis=0, keepdims=True))
                    inverse.append(1.0 / jnp.sum(p, axis=0, keepdims=True))
                    p = p.astype(BF16)
                    probs.append(
                        jnp.concatenate([jnp.where(first, p, zero), jnp.where(first, zero, p)], axis=0)
                    )
            out = []
            for h in range(0, heads, 2):
                o = nn(
                    v_t[h * head_dim : (h + 2) * head_dim],
                    jnp.concatenate(probs[h : h + 2], axis=1),
                )
                out.append(o[:head_dim, :LANES] * inverse[h])
                out.append(o[head_dim:, LANES:] * inverse[h + 1])
            mixed.append(jnp.concatenate(out, axis=0))
        mix = jnp.concatenate(mixed, axis=1).astype(BF16)
        at = g * GROUP * qtok
        return nn(wot[...], mix) + raw[:, at : at + GROUP * qtok].astype(F32)

    def feed_forward(g, s1):
        c = s1 - jnp.mean(s1, axis=0, keepdims=True)
        v = jnp.mean(c * c, axis=0, keepdims=True)
        n2 = (c * lax.rsqrt(v + 1e-05)).astype(BF16)
        total = s1
        step = 2 * LANES
        for i in range(0, ff_loc * parts, step):
            act = gelu(nn(wup[i : i + step], n2)).astype(BF16)
            total = total + nn(wdt[:, i : i + step], act)
        f = tn(total.astype(BF16), hw[...])
        for w in range(GROUP):
            at = (g * GROUP + w) * WLON
            fscr[:, :, at : at + WLON, :] = f[w * qtok : (w + 1) * qtok].reshape(
                levs, half, WLON, width
            )

    for g in range(windows // GROUP):
        feed_forward(g, attention(g))

    patches = half * (cols // dests)
    for lev in range(levs):
        f = fscr[lev].reshape(half * cols, width).astype(BF16)
        o = tn(f, perm[...]).astype(BF16)
        for d in range(dests):
            outs[d][lev] = o[:, d * patches : (d + 1) * patches]


def forecast(n_win, raw, hw, perm, a_parts, b_parts, *, side, dests, levs, n_rows, heads_loc):
    windows, wtok, feats = n_win.shape
    cols = windows * WLON
    half = n_rows // 2
    parts = len(a_parts)
    head_dim = feats // (heads_loc * parts)
    e_loc = heads_loc * head_dim
    width = hw.shape[1]
    ff_loc = (b_parts[0].shape[0] - e_loc * 3 // 2) * 2 * LANES // (3 * LANES + 2 * feats)
    heads = heads_loc * parts
    patches = half * (cols // dests)
    vm = pl.BlockSpec(memory_space=pltpu.VMEM)
    return pl.pallas_call(
        functools.partial(
            forecast_kernel,
            side=side,
            parts=parts,
            dests=dests,
            e_loc=e_loc,
            heads_loc=heads_loc,
            ff_loc=ff_loc,
            levs=levs,
            n_rows=n_rows,
        ),
        out_shape=[VMEM((levs, width, patches), BF16)] * dests,
        in_specs=[vm] * (4 + 2 * parts),
        out_specs=[vm] * dests,
        scratch_shapes=[
            pltpu.VMEM((feats, feats), BF16),
            pltpu.VMEM((feats, feats), BF16),
            pltpu.VMEM((feats, feats), BF16),
            pltpu.VMEM((feats, feats), BF16),
            pltpu.VMEM((ff_loc * parts, feats), BF16),
            pltpu.VMEM((feats, ff_loc * parts), BF16),
            pltpu.VMEM((wtok, heads * LANES), F32),
            pltpu.VMEM((levs, half, cols, width), F32),
        ],
        compiler_params=PARAMS,
    )(*map(near, (n_win, raw, hw, perm, *a_parts, *b_parts)))


def analysis_kernel(*refs, members, side):
    x_refs = refs[:members]
    idx, weight, value = refs[members : members + 3]
    out = refs[-1]
    levs, width, patches = x_refs[0].shape
    slots = idx.shape[1]
    half, cw = out.shape[2], out.shape[3]
    xs = [[x_refs[m][lev].astype(F32) for lev in range(levs)] for m in range(members)]
    state = lax.broadcasted_iota(jnp.int32, (width, patches), 0)
    pairs = [(i, k) for i in range(members) for k in range(i, members)]
    mat = {p: None for p in pairs}
    rhs = [None] * members
    for k in range(slots):
        at = idx[0, k : k + 1]
        hits = [state + lev * width == at for lev in range(levs)]
        y = []
        for m in range(members):
            total = jnp.where(hits[0], xs[m][0], 0.0)
            for lev in range(1, levs):
                total = jnp.where(hits[lev], xs[m][lev], total)
            y.append(jnp.sum(total, axis=0, keepdims=True))
        y_mean = sum(y[1:], y[0]) * (1.0 / members)
        yp = [v - y_mean for v in y]
        r = weight[0, k : k + 1]
        d = value[0, k : k + 1] - y_mean
        for i in range(members):
            ry = r * yp[i]
            for n in range(i, members):
                t = ry * yp[n]
                mat[i, n] = t if k == 0 else mat[i, n] + t
            t = ry * d
            rhs[i] = t if k == 0 else rhs[i] + t
    for i in range(members):
        mat[i, i] = mat[i, i] + (members - 1.0)
    trace = sum([mat[i, i] for i in range(1, members)], mat[0, 0])
    inv = 1.0 / trace

    def entry(a, i, n):
        return a[pairs.index((min(i, n), max(i, n)))]

    def times(a, b):
        res = []
        for i, n in pairs:
            acc = entry(a, i, 0) * entry(b, 0, n)
            for q in range(1, members):
                acc = acc + entry(a, i, q) * entry(b, q, n)
            res.append(acc)
        return res

    def sweep(_, carry):
        g, z = carry
        zg = times(z, g)
        f = [(1.5 if i == n else 0.0) - 0.5 * v for (i, n), v in zip(pairs, zg)]
        return times(g, f), times(f, z)

    g0 = [mat[p] * inv for p in pairs]
    z0 = [jnp.full_like(trace, 1.0 if i == n else 0.0) for i, n in pairs]
    _, z = lax.fori_loop(0, NEWTON, sweep, (g0, z0))
    zz = times(z, z)
    root = math.sqrt(members - 1.0) * lax.rsqrt(trace)
    mean_w = []
    for i in range(members):
        acc = entry(zz, i, 0) * rhs[0]
        for n in range(1, members):
            acc = acc + entry(zz, i, n) * rhs[n]
        mean_w.append(acc * inv)
    me = lax.axis_index("member")
    centers, spreads = [], []
    for lev in range(levs):
        total = xs[0][lev]
        for m in range(1, members):
            total = total + xs[m][lev]
        c = total * (1.0 / members)
        centers.append(c)
        spreads.append([xs[m][lev] - c for m in range(members)])
    for m in range(members):
        w = [mean_w[i] + root * entry(z, i, m) for i in range(members)]
        for lev in range(levs):
            acc = centers[lev]
            for i in range(members):
                acc = acc + spreads[lev][i] * w[i]
            out[m ^ me, lev] = acc.T.reshape(half, cw, width)


def analysis(xs, idx, weight, value, out_shape, side, prev):
    members = len(xs)
    levs, width, patches = xs[0].shape
    _, _, n_rows, cw, _ = out_shape
    half = n_rows // 2
    slots = idx.shape[1]
    vm = pl.BlockSpec(memory_space=pltpu.VMEM)
    obs = pl.BlockSpec((1, slots, patches), lambda i: (side, 0, 0))
    args = [*map(near, (*xs, idx, weight, value))]
    specs = [pl.BlockSpec((levs, width, patches), lambda i: (0, 0, 0))] * members + [obs] * 3
    aliases = {}
    if prev is not None:
        aliases = {len(args): 0}
        args.append(prev)
        specs.append(pl.BlockSpec(memory_space=pl.ANY))
    del vm
    return pl.pallas_call(
        functools.partial(analysis_kernel, members=members, side=side),
        grid=(1,),
        out_shape=jax.ShapeDtypeStruct(out_shape, F32),
        in_specs=specs,
        out_specs=pl.BlockSpec((members, levs, half, cw, width), lambda i: (0, 0, side, 0, 0)),
        input_output_aliases=aliases,
        compiler_params=PARAMS,
    )(*args)


def from_others(array, axis):
    size = lax.axis_size(axis)
    return [array] + [
        lax.ppermute(array, axis, [(i, (i + s) % size) for i in range(size)])
        for s in range(1, size)
    ]


def shards(
    prior_grids,
    w_qkv,
    w_out,
    w_up,
    w_down,
    head_weight,
    pos_bias,
    zonal_offsets,
    obs_index,
    obs_count,
    obs_value,
    obs_weight,
):
    member_grid = prior_grids[0]
    levs = member_grid.shape[0] // lax.axis_size("tensor")
    n_rows = member_grid.shape[1]
    dests = lax.axis_size("member")
    bands = lax.axis_size("band")
    heads_loc = pos_bias.shape[0]

    prior_t = member_grid.swapaxes(2, 3)
    half = n_rows // 2
    mine = lax.dynamic_slice_in_dim(prior_t, lax.axis_index("tensor") * levs, levs, 0)
    up = [(i, i + 1) for i in range(bands - 1)]
    above = lax.ppermute(mine[:, half:], "band", up)
    below = lax.ppermute(mine[:, :half], "band", [(b, a) for a, b in up])
    a_mine, b_mine = pack(w_qkv.transpose(1, 0, 2), w_out, w_up, w_down.T, pos_bias)
    a_parts = from_others(a_mine, "tensor")
    b_parts = from_others(b_mine, "tensor")
    obs = (
        obs_index[0].swapaxes(1, 2),
        obs_count[0],
        obs_value[0].swapaxes(1, 2),
        obs_weight[0].swapaxes(1, 2),
    )
    n_0, n_1, raw_0, raw_1, hw, perm, idx, value, weight = prologue(
        zonal_offsets, prior_t, above, below, head_weight.T, obs, levs, dests
    )
    cw = obs_index.shape[2]

    received = []
    for side, n_win, raw in ((0, n_0, raw_0), (1, n_1, raw_1)):
        if received:
            n_win, _ = lax.optimization_barrier((n_win, received[0][0]))
        sent = forecast(
            n_win,
            raw,
            hw,
            perm,
            a_parts,
            b_parts,
            side=side,
            dests=dests,
            levs=levs,
            n_rows=n_rows,
            heads_loc=heads_loc,
        )
        pieces = [sent[0]]
        for k in range(1, dests):
            pieces.append(lax.ppermute(sent[k], "member", [(i, i ^ k) for i in range(dests)]))
        received.append(pieces)
    out_shape = (dests, levs, n_rows, cw, head_weight.shape[1])
    result = None
    for side in range(2):
        result = analysis(received[side], idx, weight, value, out_shape, side, result)
    return result


def solution(mesh):
    return jax.shard_map(
        shards,
        mesh=mesh,
        in_specs=(
            P("member", None, "band", None, None),
            P(None, None, "tensor"),
            P("tensor", None),
            P(None, "tensor"),
            P("tensor", None),
            P(),
            P("tensor", None, None),
            P("member"),
            P("tensor", "band", "member", None),
            P("tensor", "band", "member"),
            P("tensor", "band", "member", None),
            P("tensor", "band", "member", None),
        ),
        out_specs=P(None, "tensor", "band", "member", None),
        check_vma=False,
    )
```

```python
import functools
import math

import jax
import jax.numpy as jnp
from jax import lax
from jax.experimental import pallas as pl
from jax.experimental.pallas import tpu as pltpu
from jax.sharding import PartitionSpec as P


WLON = 8
NEWTON = 8
LANES = 128
GROUP = 4
LOG2E = 1.4426950408889634
F32 = jnp.float32
BF16 = jnp.bfloat16


VMEM = pltpu.VMEM
PARAMS = pltpu.CompilerParams(vmem_limit_bytes=32 * 1024 * 1024)


def near(x):
    return pltpu.with_memory_space_constraint(x, pltpu.VMEM)


def far(x):
    return pltpu.with_memory_space_constraint(x, pltpu.HBM)


def nn(a, b):
    return lax.dot_general(a, b, (((1,), (0,)), ((), ())), preferred_element_type=F32)


def nt(a, b):
    return lax.dot_general(a, b, (((1,), (1,)), ((), ())), preferred_element_type=F32)


def tn(a, b):
    return lax.dot_general(a, b, (((0,), (0,)), ((), ())), preferred_element_type=F32)


def eye(n):
    return (
        lax.broadcasted_iota(jnp.int32, (n, n), 0) == lax.broadcasted_iota(jnp.int32, (n, n), 1)
    ).astype(BF16)


def to_dense(x):
    half = x.shape[0] // 2
    return jnp.concatenate(
        [x[:, :LANES], jnp.concatenate([x[:half, LANES:], x[half:, LANES:]], axis=1)], axis=0
    )


def from_dense(d):
    rows = d.shape[0] * 2 // 3
    half = rows // 2
    part = LANES // 2
    high = jnp.concatenate([d[rows:, :part], d[rows:, part:]], axis=0)
    del half
    return jnp.concatenate([d[:rows], high], axis=1)


def pack_kernel(prior, *refs):
    weights, (full, half, own, top, bot), (*local, sems) = refs[:5], refs[5:10], refs[10:]
    levs, n_rows, feats, _ = own.shape
    mid = n_rows // 2
    here = pl.ds(lax.axis_index("tensor") * levs, levs)
    loads = [
        pltpu.make_async_copy(src, dst, sems.at[i])
        for i, (src, dst) in enumerate(zip(weights, local))
    ]
    copies = [
        pltpu.make_async_copy(prior.at[here, :mid], top, sems.at[5]),
        pltpu.make_async_copy(prior.at[here, mid:], bot, sems.at[6]),
        pltpu.make_async_copy(prior.at[here], own, sems.at[7]),
    ]
    for copy in loads + copies:
        copy.start()
    for copy in loads:
        copy.wait()
    qkv, w_out, w_up, w_down, bias = local
    ident = eye(qkv.shape[2])
    dense = to_dense(jnp.concatenate([nt(ident, qkv[i]).astype(BF16) for i in range(3)], axis=0))
    at = dense.shape[0]
    full[:at] = dense
    heads, wtok, _ = bias.shape
    for h in range(heads):
        full[at + h * wtok : at + (h + 1) * wtok] = bias[h]
    at += heads * wtok
    for piece in (to_dense(w_out[...]), to_dense(nt(eye(w_up.shape[1]), w_up[...]).astype(BF16))):
        full[at : at + piece.shape[0]] = piece
        at += piece.shape[0]
    for i in range(w_down.shape[1] // LANES):
        full[at : at + feats] = w_down[:, i * LANES : (i + 1) * LANES]
        at += feats
    rows = half.shape[0]
    mine = lax.axis_index("band") % 2
    half[...] = full[pl.ds(pl.multiple_of(mine * rows, 16), rows)]
    for copy in copies:
        copy.wait()


def pack(prior_t, qkv, w_out, w_up, w_down, bias, levs):
    _, n_rows, feats, cols = prior_t.shape
    e_loc = qkv.shape[2]
    heads, wtok, _ = bias.shape
    ff = w_up.shape[1]
    rows = 3 * e_loc * 3 // 2 + heads * wtok + e_loc * 3 // 2 + ff * 3 // 2 + feats * (ff // LANES)
    vm = pl.BlockSpec(memory_space=pltpu.VMEM)
    edge = VMEM((levs, n_rows // 2, feats, cols), BF16)
    return pl.pallas_call(
        pack_kernel,
        out_shape=(
            VMEM((rows, LANES), BF16),
            VMEM((rows // 2, LANES), BF16),
            VMEM((levs, n_rows, feats, cols), BF16),
            edge,
            edge,
        ),
        in_specs=[pl.BlockSpec(memory_space=pltpu.HBM)] * 6,
        out_specs=[vm] * 5,
        scratch_shapes=[VMEM(w.shape, BF16) for w in (qkv, w_out, w_up, w_down, bias)]
        + [pltpu.SemaphoreType.DMA((8,))],
        compiler_params=PARAMS,
        name="pack",
    )(*map(far, (prior_t, qkv, w_out, w_up, w_down, bias)))


def roll_matrix(off, cols):
    j = lax.broadcasted_iota(jnp.int32, (cols, cols), 0) + off
    j = jnp.where(j >= cols, j - cols, j)
    return (j == lax.broadcasted_iota(jnp.int32, (cols, cols), 1)).astype(BF16)


def norm_rows(x):
    feats = x.shape[0]
    x = x.astype(F32)
    c = x - jnp.sum(x, axis=0, keepdims=True) * (1.0 / feats)
    v = jnp.sum(c * c, axis=0, keepdims=True) * (1.0 / feats)
    return (c * lax.rsqrt(v + 1e-05)).astype(BF16)


def by_window(first, second):
    cols, feats = first.shape
    f = first.reshape(cols // WLON, 1, WLON, feats)
    s = second.reshape(cols // WLON, 1, WLON, feats)
    both = jnp.concatenate([f, s], axis=1)
    return both.reshape(cols // WLON, 2 * WLON, feats).astype(BF16)


def own_kernel(offs, own, hw_t, obs_i, obs_n, obs_v, obs_w, *refs):
    n_refs, raw_refs, hw, perm, idx, val, wgt, xscr = refs[:2], refs[2:4], *refs[4:]
    levs, n_rows, feats, cols = own.shape
    half = n_rows // 2
    windows = cols // WLON
    off = offs[0]
    me = lax.axis_index("member")
    dests = lax.axis_size("member")
    hw[...] = nt(eye(feats), hw_t[...]).astype(BF16)

    slot = lax.broadcasted_iota(jnp.int32, obs_i.shape[1:], 0)
    for side in range(2):
        at = range(side * half, (side + 1) * half)
        idx[side] = jnp.concatenate([obs_i[r] for r in at], axis=1)
        val[side] = jnp.concatenate([obs_v[r] for r in at], axis=1)
        wgt[side] = jnp.concatenate(
            [jnp.where(slot < obs_n[r : r + 1], obs_w[r], 0.0) for r in at], axis=1
        )

    cw = cols // dests
    patches = half * cw
    lane = lax.broadcasted_iota(jnp.int32, (cols, LANES), 1)
    col = lax.broadcasted_iota(jnp.int32, (cols, LANES), 0) + off
    col = jnp.where(col >= cols, col - cols, col)
    dest = col // cw
    base = (dest ^ me) * patches + (col - dest * cw)
    for r in range(half):
        for b in range(dests * patches // LANES):
            hit = base + r * cw == lane + b * LANES
            perm[r * cols : (r + 1) * cols, b * LANES : (b + 1) * LANES] = hit.astype(BF16)

    rollm = roll_matrix(off, cols)
    qtok = levs * half * WLON
    ident = eye(feats)
    for side in range(2):

        def one_level(lev, carry, side=side):
            for r in range(0, half, 2):
                x0, x1 = own[lev, side * half + r], own[lev, side * half + r + 1]
                n_refs[side][:, lev, r * WLON : (r + 2) * WLON, :] = by_window(
                    nt(rollm, norm_rows(x0)), nt(rollm, norm_rows(x1))
                )
                xscr[:, lev, r * WLON : (r + 2) * WLON, :] = by_window(
                    nt(rollm, x0), nt(rollm, x1)
                )
            return carry

        lax.fori_loop(0, levs, one_level, 0)
        for w in range(0, windows, GROUP):
            x = xscr[w : w + GROUP].reshape(GROUP * qtok, feats)
            raw_refs[side][:, w * qtok : (w + GROUP) * qtok] = nt(ident, x).astype(BF16)


def prepare_own(offs, own, hw_t, obs, dests):
    levs, n_rows, feats, cols = own.shape
    slots = obs[0].shape[1]
    half = n_rows // 2
    patches = half * (cols // dests)
    windows = cols // WLON
    width = hw_t.shape[0]
    n_shape = VMEM((windows, levs, half * WLON, feats), BF16)
    raw_shape = VMEM((feats, levs * half * cols), BF16)
    vm = pl.BlockSpec(memory_space=pltpu.VMEM)
    return pl.pallas_call(
        own_kernel,
        out_shape=(
            n_shape,
            n_shape,
            raw_shape,
            raw_shape,
            VMEM((feats, width), BF16),
            VMEM((half * cols, half * cols), BF16),
            VMEM((2, slots, patches), jnp.int32),
            VMEM((2, slots, patches), F32),
            VMEM((2, slots, patches), F32),
        ),
        in_specs=[pl.BlockSpec(memory_space=pltpu.SMEM)] + [vm] * 6,
        out_specs=[vm] * 9,
        scratch_shapes=[VMEM(n_shape.shape, BF16)],
        compiler_params=PARAMS,
        name="prepare_own",
    )(offs, near(own), near(hw_t), *map(near, obs))


def halo_kernel(offs, above, below, *n_refs):
    levs, half, _, cols = above.shape
    rollm = roll_matrix(offs[0], cols)
    for side, halo in enumerate((above, below)):

        def one_level(lev, carry, side=side, halo=halo):
            for r in range(0, half, 2):
                n_refs[side][:, lev, r * WLON : (r + 2) * WLON, :] = by_window(
                    nt(rollm, norm_rows(halo[lev, r])), nt(rollm, norm_rows(halo[lev, r + 1]))
                )
            return carry

        lax.fori_loop(0, levs, one_level, 0)


def prepare_halo(offs, above, below):
    levs, half, feats, cols = above.shape
    vm = pl.BlockSpec(memory_space=pltpu.VMEM)
    return pl.pallas_call(
        halo_kernel,
        out_shape=[VMEM((cols // WLON, levs, half * WLON, feats), BF16)] * 2,
        in_specs=[pl.BlockSpec(memory_space=pltpu.SMEM), vm, vm],
        out_specs=[vm] * 2,
        compiler_params=PARAMS,
        name="prepare_halo",
    )(offs, near(above), near(below))


def forecast_kernel(*refs, side, dests, e_loc, heads_loc, ff_loc):
    n_halo, n_own, raw, hw, perm, mine, got, passed = refs[:8]
    outs = refs[8 : 8 + dests]
    (wq, wk, wv, wot, wup, wdt, bias, fscr, theirs) = refs[8 + dests :]
    windows, levs, span, feats = n_own.shape
    half = span // WLON
    n_rows = 2 * half
    wtok = levs * n_rows * WLON
    parts = 2
    cols = windows * WLON
    qtok = levs * half * WLON
    heads = heads_loc * parts
    head_dim = e_loc // heads_loc
    width = hw.shape[1]
    q_row = half - half * side
    band = lax.axis_index("band")
    if side == 0:
        is_open = band > 0
    else:
        is_open = band < lax.axis_size("band") - 1
    penalty = jnp.where(is_open, 0.0, -1000000000.0).astype(F32)

    rows = got.shape[0]
    theirs[pl.ds(pl.multiple_of((band % 2) * rows, 16), rows)] = got[...]
    theirs[pl.ds(pl.multiple_of((1 - band % 2) * rows, 16), rows)] = passed[...]
    w_parts = (mine, theirs)
    n_a = 3 * e_loc * 3 // 2
    n_b = n_a + heads_loc * wtok
    r0 = n_b + e_loc * 3 // 2
    r1 = r0 + ff_loc * 3 // 2
    for p in range(parts):
        qkv = from_dense(w_parts[p][:n_a])
        rows = slice(p * e_loc, (p + 1) * e_loc)
        wq[rows] = qkv[:e_loc]
        wk[rows] = qkv[e_loc : 2 * e_loc]
        wv[rows] = qkv[2 * e_loc :]
        wup[p * ff_loc : (p + 1) * ff_loc] = from_dense(w_parts[p][r0:r1])
        for i in range(ff_loc // LANES):
            lo = p * ff_loc + i * LANES
            down = w_parts[p][r1 + i * feats : r1 + (i + 1) * feats].astype(F32) * 0.5
            wdt[:, lo : lo + LANES] = down.astype(BF16)
    w_out = jnp.concatenate([from_dense(w_parts[p][n_b:r0]) for p in range(parts)], axis=0)
    wot[...] = tn(w_out, eye(heads * head_dim)).astype(BF16)

    lat = (lax.broadcasted_iota(jnp.int32, (wtok, 1), 0) // WLON) % n_rows
    closed = (lat < half) if side == 0 else (lat >= half)
    shut = jnp.where(closed, penalty, 0.0)
    for p in range(parts):
        for h in range(heads_loc):
            rows = []
            for lev in range(levs):
                lo = n_a + h * wtok + lev * n_rows * WLON + q_row * WLON
                rows.append(w_parts[p][lo : lo + span].astype(F32))
            at = (p * heads_loc + h) * LANES
            bias[:, at : at + LANES] = (
                jnp.concatenate(rows * (LANES // qtok), axis=0).T * LOG2E + shut
            )

    first = lax.broadcasted_iota(jnp.int32, (1, LANES), 1) < qtok
    zero = jnp.zeros((), BF16)
    q_scale = head_dim**-0.5 * LOG2E
    e_all = heads * head_dim

    def zeros(rows):
        return jnp.zeros((rows, LANES), BF16)

    s1 = {}

    def attention(g):
        x_q = n_own[g * GROUP : (g + 1) * GROUP]
        x_h = n_halo[g * GROUP : (g + 1) * GROUP]
        order = [x_h, x_q] if side == 0 else [x_q, x_h]
        x_all = jnp.concatenate(order, axis=2).reshape(GROUP * wtok, feats)
        q_all = (nt(wq[...], x_q.reshape(GROUP * qtok, feats)) * q_scale).astype(BF16)
        k_all = nt(x_all, wk[...])
        v_all = nt(wv[...], x_all).astype(BF16)
        yield
        mixed = []
        for pair in range(GROUP // 2):
            k0 = k_all[2 * pair * wtok : (2 * pair + 1) * wtok]
            k1 = k_all[(2 * pair + 1) * wtok : (2 * pair + 2) * wtok]
            q_t = q_all[:, pair * LANES : (pair + 1) * LANES]
            qa = jnp.where(first, q_t, zero)
            qb = jnp.where(first, zero, q_t)
            v_t = v_all[:, 2 * pair * wtok : (2 * pair + 2) * wtok]
            out = []
            for e0 in range(0, e_all, LANES):
                dims = min(LANES, e_all - e0)
                lhs = jnp.concatenate([k0[:, e0 : e0 + dims], k1[:, e0 : e0 + dims]], axis=1)
                columns = []
                for h in range(dims // head_dim):
                    a = e0 + h * head_dim
                    gaps = (h * head_dim, dims - (h + 1) * head_dim)
                    col = []
                    for q in (qa, qb):
                        if gaps[0]:
                            col.append(zeros(gaps[0]))
                        col.append(q[a : a + head_dim])
                        if gaps[1]:
                            col.append(zeros(gaps[1]))
                    columns.append(jnp.concatenate(col, axis=0))
                s = nn(lhs.astype(BF16), jnp.concatenate(columns, axis=1))
                yield
                for h in range(0, dims // head_dim, 2):
                    probs, inverse = [], []
                    for n in (h, h + 1):
                        at = (e0 // head_dim + n) * LANES
                        t = s[:, n * LANES : (n + 1) * LANES] + bias[:, at : at + LANES]
                        p = jnp.exp2(t - jnp.max(t, axis=0, keepdims=True))
                        inverse.append(1.0 / jnp.sum(p, axis=0, keepdims=True))
                        p = p.astype(BF16)
                        probs.append(
                            jnp.concatenate(
                                [jnp.where(first, p, zero), jnp.where(first, zero, p)], axis=0
                            )
                        )
                    a = e0 + h * head_dim
                    o = nn(v_t[a : a + 2 * head_dim], jnp.concatenate(probs, axis=1))
                    out.append(o[:head_dim, :LANES] * inverse[0])
                    out.append(o[head_dim:, LANES:] * inverse[1])
                    yield
            mixed.append(jnp.concatenate(out, axis=0).astype(BF16))
        at = g * GROUP * qtok
        mix = jnp.concatenate(mixed, axis=1)
        s1[g] = nn(wot[...], mix) + raw[:, at : at + GROUP * qtok].astype(F32)
        yield

    def feed_forward(g):
        x = s1.pop(g)
        c = x - jnp.mean(x, axis=0, keepdims=True)
        v = jnp.mean(c * c, axis=0, keepdims=True)
        n2 = (c * lax.rsqrt(v + 1e-05)).astype(BF16)
        yield
        total = x
        step = 2 * LANES
        for i in range(0, ff_loc * parts, step):
            up = nn(wup[i : i + step], n2)
            yield
            act = (up + up * lax.erf(up * math.sqrt(0.5))).astype(BF16)
            total = total + nn(wdt[:, i : i + step], act)
            yield
        f = tn(total.astype(BF16), hw[...])
        yield
        for w in range(GROUP):
            at = (g * GROUP + w) * WLON
            fscr[:, :, at : at + WLON, :] = f[w * qtok : (w + 1) * qtok].reshape(
                levs, half, WLON, width
            )
        yield

    groups = windows // GROUP
    for g in range(groups + 1):
        tasks = []
        if g:
            tasks.append(feed_forward(g - 1))
        if g < groups:
            tasks.append(attention(g))
        while tasks:
            for task in list(tasks):
                if next(task, tasks) is tasks:
                    tasks.remove(task)

    patches = half * (cols // dests)
    for lev in range(levs):
        f = fscr[lev].reshape(half * cols, width).astype(BF16)
        o = tn(f, perm[...]).astype(BF16)
        for d in range(dests):
            outs[d][lev] = o[:, d * patches : (d + 1) * patches]


def forecast(n_halo, n_own, raw, hw, perm, weights, *, side, dests, heads_loc):
    windows, levs, span, feats = n_own.shape
    cols = windows * WLON
    half = span // WLON
    parts = 2
    head_dim = feats // (heads_loc * parts)
    e_loc = heads_loc * head_dim
    width = hw.shape[1]
    wtok = 2 * levs * span
    rows = weights[0].shape[0] - 4 * (e_loc * 3 // 2) - heads_loc * wtok
    ff_loc = rows * 2 * LANES // (3 * LANES + 2 * feats)
    heads = heads_loc * parts
    patches = half * (cols // dests)
    vm = pl.BlockSpec(memory_space=pltpu.VMEM)
    return pl.pallas_call(
        functools.partial(
            forecast_kernel,
            side=side,
            dests=dests,
            e_loc=e_loc,
            heads_loc=heads_loc,
            ff_loc=ff_loc,
        ),
        out_shape=[VMEM((levs, width, patches), BF16)] * dests,
        in_specs=[vm] * 8,
        out_specs=[vm] * dests,
        scratch_shapes=[
            pltpu.VMEM((feats, feats), BF16),
            pltpu.VMEM((feats, feats), BF16),
            pltpu.VMEM((feats, feats), BF16),
            pltpu.VMEM((feats, feats), BF16),
            pltpu.VMEM((ff_loc * parts, feats), BF16),
            pltpu.VMEM((feats, ff_loc * parts), BF16),
            pltpu.VMEM((wtok, heads * LANES), F32),
            pltpu.VMEM((levs, half, cols, width), F32),
            pltpu.VMEM(weights[0].shape, BF16),
        ],
        compiler_params=PARAMS,
    )(*map(near, (n_halo, n_own, raw, hw, perm, *weights)))


def analysis_kernel(*refs, members, side):
    x_refs = refs[:members]
    idx, weight, value = refs[members : members + 3]
    out = refs[-1]
    levs, width, patches = x_refs[0].shape
    slots = idx.shape[1]
    half, cw = out.shape[2], out.shape[3]
    xs = [[x_refs[m][lev].astype(F32) for lev in range(levs)] for m in range(members)]
    state = lax.broadcasted_iota(jnp.int32, (width, patches), 0)
    pairs = [(i, k) for i in range(members) for k in range(i, members)]
    mat = {p: None for p in pairs}
    rhs = [None] * members
    for k in range(slots):
        at = idx[0, k : k + 1]
        hits = [state + lev * width == at for lev in range(levs)]
        y = []
        for m in range(members):
            total = jnp.where(hits[0], xs[m][0], 0.0)
            for lev in range(1, levs):
                total = jnp.where(hits[lev], xs[m][lev], total)
            y.append(jnp.sum(total, axis=0, keepdims=True))
        y_mean = sum(y[1:], y[0]) * (1.0 / members)
        yp = [v - y_mean for v in y]
        r = weight[0, k : k + 1]
        d = value[0, k : k + 1] - y_mean
        for i in range(members):
            ry = r * yp[i]
            for n in range(i, members):
                t = ry * yp[n]
                mat[i, n] = t if k == 0 else mat[i, n] + t
            t = ry * d
            rhs[i] = t if k == 0 else rhs[i] + t
    for i in range(members):
        mat[i, i] = mat[i, i] + (members - 1.0)
    trace = sum([mat[i, i] for i in range(1, members)], mat[0, 0])
    inv = 1.0 / trace

    def entry(a, i, n):
        return a[pairs.index((min(i, n), max(i, n)))]

    def times(a, b):
        res = []
        for i, n in pairs:
            acc = entry(a, i, 0) * entry(b, 0, n)
            for q in range(1, members):
                acc = acc + entry(a, i, q) * entry(b, q, n)
            res.append(acc)
        return res

    def sweep(_, carry):
        g, z = carry
        zg = times(z, g)
        f = [(1.5 if i == n else 0.0) - 0.5 * v for (i, n), v in zip(pairs, zg)]
        return times(g, f), times(f, z)

    g0 = [mat[p] * inv for p in pairs]
    z0 = [jnp.full_like(trace, 1.0 if i == n else 0.0) for i, n in pairs]
    _, z = lax.fori_loop(0, NEWTON, sweep, (g0, z0))
    zz = times(z, z)
    root = math.sqrt(members - 1.0) * lax.rsqrt(trace)
    mean_w = []
    for i in range(members):
        acc = entry(zz, i, 0) * rhs[0]
        for n in range(1, members):
            acc = acc + entry(zz, i, n) * rhs[n]
        mean_w.append(acc * inv)
    me = lax.axis_index("member")
    centers, spreads = [], []
    for lev in range(levs):
        total = xs[0][lev]
        for m in range(1, members):
            total = total + xs[m][lev]
        c = total * (1.0 / members)
        centers.append(c)
        spreads.append([xs[m][lev] - c for m in range(members)])
    for m in range(members):
        w = [mean_w[i] + root * entry(z, i, m) for i in range(members)]
        for lev in range(levs):
            acc = centers[lev]
            for i in range(members):
                acc = acc + spreads[lev][i] * w[i]
            out[m ^ me, lev] = acc.T.reshape(half, cw, width)


def analysis(xs, idx, weight, value, out_shape, side, prev):
    members = len(xs)
    levs, width, patches = xs[0].shape
    _, _, n_rows, cw, _ = out_shape
    half = n_rows // 2
    slots = idx.shape[1]
    vm = pl.BlockSpec(memory_space=pltpu.VMEM)
    obs = pl.BlockSpec((1, slots, patches), lambda i: (side, 0, 0))
    args = [*map(near, (*xs, idx, weight, value))]
    specs = [pl.BlockSpec((levs, width, patches), lambda i: (0, 0, 0))] * members + [obs] * 3
    aliases = {}
    if prev is not None:
        aliases = {len(args): 0}
        args.append(prev)
        specs.append(pl.BlockSpec(memory_space=pl.ANY))
    del vm
    return pl.pallas_call(
        functools.partial(analysis_kernel, members=members, side=side),
        grid=(1,),
        out_shape=jax.ShapeDtypeStruct(out_shape, F32),
        in_specs=specs,
        out_specs=pl.BlockSpec((members, levs, half, cw, width), lambda i: (0, 0, side, 0, 0)),
        input_output_aliases=aliases,
        compiler_params=PARAMS,
    )(*args)


def shards(
    prior_grids,
    w_qkv,
    w_out,
    w_up,
    w_down,
    head_weight,
    pos_bias,
    zonal_offsets,
    obs_index,
    obs_count,
    obs_value,
    obs_weight,
):
    member_grid = prior_grids[0]
    levs = member_grid.shape[0] // lax.axis_size("tensor")
    n_rows = member_grid.shape[1]
    dests = lax.axis_size("member")
    bands = lax.axis_size("band")
    heads_loc = pos_bias.shape[0]

    prior_t = member_grid.swapaxes(2, 3)
    sides = lax.axis_size("tensor")
    mine, piece, own, top, bottom = pack(
        prior_t, w_qkv.transpose(1, 0, 2), w_out, w_up, w_down.T, pos_bias, levs
    )
    got = lax.ppermute(piece, "tensor", [(i, (i + 1) % sides) for i in range(sides)])
    up = [(i, i + 1) for i in range(bands - 1)]
    above = lax.ppermute(bottom, "band", up)
    below = lax.ppermute(top, "band", [(b, a) for a, b in up])
    passed = lax.ppermute(got, "band", [(i, i ^ 1) for i in range(bands)])
    obs = (
        obs_index[0].swapaxes(1, 2),
        obs_count[0],
        obs_value[0].swapaxes(1, 2),
        obs_weight[0].swapaxes(1, 2),
    )
    n_own_0, n_own_1, raw_0, raw_1, hw, perm, idx, value, weight = prepare_own(
        zonal_offsets, own, head_weight.T, obs, dests
    )
    n_halo_0, n_halo_1 = prepare_halo(zonal_offsets, above, below)
    cw = obs_index.shape[2]

    received = []
    for side, n_halo, n_own, raw in ((0, n_halo_0, n_own_0, raw_0), (1, n_halo_1, n_own_1, raw_1)):
        if received:
            n_own, _ = lax.optimization_barrier((n_own, received[0][0]))
        sent = forecast(
            n_halo,
            n_own,
            raw,
            hw,
            perm,
            (mine, got, passed),
            side=side,
            dests=dests,
            heads_loc=heads_loc,
        )
        pieces = [sent[0]]
        for k in range(1, dests):
            pieces.append(lax.ppermute(sent[k], "member", [(i, i ^ k) for i in range(dests)]))
        received.append(pieces)
    out_shape = (dests, levs, n_rows, cw, head_weight.shape[1])
    result = None
    for side in range(2):
        result = analysis(received[side], idx, weight, value, out_shape, side, result)
    return result


def solution(mesh):
    return jax.shard_map(
        shards,
        mesh=mesh,
        in_specs=(
            P("member", None, "band", None, None),
            P(None, None, "tensor"),
            P("tensor", None),
            P(None, "tensor"),
            P("tensor", None),
            P(),
            P("tensor", None, None),
            P("member"),
            P("tensor", "band", "member", None),
            P("tensor", "band", "member"),
            P("tensor", "band", "member", None),
            P("tensor", "band", "member", None),
        ),
        out_specs=P(None, "tensor", "band", "member", None),
        check_vma=False,
    )
```

```python
import functools
import math

import jax
import jax.numpy as jnp
from jax import lax
from jax.experimental import pallas as pl
from jax.experimental.pallas import tpu as pltpu
from jax.sharding import PartitionSpec as P


WLON = 8
NEWTON = 8
LANES = 128
GROUP = 4
LOG2E = 1.4426950408889634
F32 = jnp.float32
BF16 = jnp.bfloat16


VMEM = pltpu.VMEM
PARAMS = pltpu.CompilerParams(vmem_limit_bytes=32 * 1024 * 1024)


def near(x):
    return pltpu.with_memory_space_constraint(x, pltpu.VMEM)


def far(x):
    return pltpu.with_memory_space_constraint(x, pltpu.HBM)


def nn(a, b):
    return lax.dot_general(a, b, (((1,), (0,)), ((), ())), preferred_element_type=F32)


def nt(a, b):
    return lax.dot_general(a, b, (((1,), (1,)), ((), ())), preferred_element_type=F32)


def tn(a, b):
    return lax.dot_general(a, b, (((0,), (0,)), ((), ())), preferred_element_type=F32)


def eye(n):
    return (
        lax.broadcasted_iota(jnp.int32, (n, n), 0) == lax.broadcasted_iota(jnp.int32, (n, n), 1)
    ).astype(BF16)


def to_dense(x):
    half = x.shape[0] // 2
    return jnp.concatenate(
        [x[:, :LANES], jnp.concatenate([x[:half, LANES:], x[half:, LANES:]], axis=1)], axis=0
    )


def from_dense(d):
    rows = d.shape[0] * 2 // 3
    half = rows // 2
    part = LANES // 2
    high = jnp.concatenate([d[rows:, :part], d[rows:, part:]], axis=0)
    del half
    return jnp.concatenate([d[:rows], high], axis=1)


def pack_kernel(prior, *refs):
    weights, (full, half, own, top, bot), (*local, sems) = refs[:5], refs[5:10], refs[10:]
    levs, n_rows, feats, _ = own.shape
    mid = n_rows // 2
    here = pl.ds(lax.axis_index("tensor") * levs, levs)
    loads = [
        pltpu.make_async_copy(src, dst, sems.at[i])
        for i, (src, dst) in enumerate(zip(weights, local))
    ]
    copies = [
        pltpu.make_async_copy(prior.at[here, :mid], top, sems.at[5]),
        pltpu.make_async_copy(prior.at[here, mid:], bot, sems.at[6]),
        pltpu.make_async_copy(prior.at[here], own, sems.at[7]),
    ]
    for copy in loads + copies:
        copy.start()
    for copy in loads:
        copy.wait()
    qkv, w_out, w_up, w_down, bias = local
    ident = eye(qkv.shape[2])
    dense = to_dense(jnp.concatenate([nt(ident, qkv[i]).astype(BF16) for i in range(3)], axis=0))
    at = dense.shape[0]
    full[:at] = dense
    heads, wtok, _ = bias.shape
    for h in range(heads):
        full[at + h * wtok : at + (h + 1) * wtok] = bias[h]
    at += heads * wtok
    for piece in (to_dense(w_out[...]), to_dense(nt(eye(w_up.shape[1]), w_up[...]).astype(BF16))):
        full[at : at + piece.shape[0]] = piece
        at += piece.shape[0]
    for i in range(w_down.shape[1] // LANES):
        full[at : at + feats] = w_down[:, i * LANES : (i + 1) * LANES]
        at += feats
    rows = half.shape[0]
    mine = lax.axis_index("band") % 2
    half[...] = full[pl.ds(pl.multiple_of(mine * rows, 16), rows)]
    for copy in copies:
        copy.wait()


def pack(prior_t, qkv, w_out, w_up, w_down, bias, levs):
    _, n_rows, feats, cols = prior_t.shape
    e_loc = qkv.shape[2]
    heads, wtok, _ = bias.shape
    ff = w_up.shape[1]
    rows = 3 * e_loc * 3 // 2 + heads * wtok + e_loc * 3 // 2 + ff * 3 // 2 + feats * (ff // LANES)
    vm = pl.BlockSpec(memory_space=pltpu.VMEM)
    edge = VMEM((levs, n_rows // 2, feats, cols), BF16)
    return pl.pallas_call(
        pack_kernel,
        out_shape=(
            VMEM((rows, LANES), BF16),
            VMEM((rows // 2, LANES), BF16),
            VMEM((levs, n_rows, feats, cols), BF16),
            edge,
            edge,
        ),
        in_specs=[pl.BlockSpec(memory_space=pltpu.HBM)] * 6,
        out_specs=[vm] * 5,
        scratch_shapes=[VMEM(w.shape, BF16) for w in (qkv, w_out, w_up, w_down, bias)]
        + [pltpu.SemaphoreType.DMA((8,))],
        compiler_params=PARAMS,
        name="pack",
    )(*map(far, (prior_t, qkv, w_out, w_up, w_down, bias)))


def roll_matrix(off, cols):
    j = lax.broadcasted_iota(jnp.int32, (cols, cols), 0) + off
    j = jnp.where(j >= cols, j - cols, j)
    return (j == lax.broadcasted_iota(jnp.int32, (cols, cols), 1)).astype(BF16)


def norm_rows(x):
    feats = x.shape[0]
    x = x.astype(F32)
    c = x - jnp.sum(x, axis=0, keepdims=True) * (1.0 / feats)
    v = jnp.sum(c * c, axis=0, keepdims=True) * (1.0 / feats)
    return (c * lax.rsqrt(v + 1e-05)).astype(BF16)


def by_window(first, second):
    cols, feats = first.shape
    f = first.reshape(cols // WLON, 1, WLON, feats)
    s = second.reshape(cols // WLON, 1, WLON, feats)
    both = jnp.concatenate([f, s], axis=1)
    return both.reshape(cols // WLON, 2 * WLON, feats).astype(BF16)


def own_kernel(offs, own, hw_t, obs_i, obs_n, obs_v, obs_w, *refs):
    n_refs, raw_refs, hw, perm, idx, val, wgt, xscr = refs[:2], refs[2:4], *refs[4:]
    levs, n_rows, feats, cols = own.shape
    half = n_rows // 2
    windows = cols // WLON
    off = offs[0]
    me = lax.axis_index("member")
    dests = lax.axis_size("member")
    hw[...] = nt(eye(feats), hw_t[...]).astype(BF16)

    slot = lax.broadcasted_iota(jnp.int32, obs_i.shape[1:], 0)
    for side in range(2):
        at = range(side * half, (side + 1) * half)
        idx[side] = jnp.concatenate([obs_i[r] for r in at], axis=1)
        val[side] = jnp.concatenate([obs_v[r] for r in at], axis=1)
        wgt[side] = jnp.concatenate(
            [jnp.where(slot < obs_n[r : r + 1], obs_w[r], 0.0) for r in at], axis=1
        )

    cw = cols // dests
    patches = half * cw
    lane = lax.broadcasted_iota(jnp.int32, (cols, LANES), 1)
    col = lax.broadcasted_iota(jnp.int32, (cols, LANES), 0) + off
    col = jnp.where(col >= cols, col - cols, col)
    dest = col // cw
    base = (dest ^ me) * patches + (col - dest * cw)
    for r in range(half):
        for b in range(dests * patches // LANES):
            hit = base + r * cw == lane + b * LANES
            perm[r * cols : (r + 1) * cols, b * LANES : (b + 1) * LANES] = hit.astype(BF16)

    rollm = roll_matrix(off, cols)
    qtok = levs * half * WLON
    ident = eye(feats)
    for side in range(2):

        for lev in range(levs):
            for r in range(0, half, 2):
                x0, x1 = own[lev, side * half + r], own[lev, side * half + r + 1]
                n_refs[side][:, lev, r * WLON : (r + 2) * WLON, :] = by_window(
                    nt(rollm, norm_rows(x0)), nt(rollm, norm_rows(x1))
                )
                xscr[:, lev, r * WLON : (r + 2) * WLON, :] = by_window(
                    nt(rollm, x0), nt(rollm, x1)
                )
        for w in range(0, windows, GROUP):
            x = xscr[w : w + GROUP].reshape(GROUP * qtok, feats)
            raw_refs[side][:, w * qtok : (w + GROUP) * qtok] = nt(ident, x).astype(BF16)


def prepare_own(offs, own, hw_t, obs, dests):
    levs, n_rows, feats, cols = own.shape
    slots = obs[0].shape[1]
    half = n_rows // 2
    patches = half * (cols // dests)
    windows = cols // WLON
    width = hw_t.shape[0]
    n_shape = VMEM((windows, levs, half * WLON, feats), BF16)
    raw_shape = VMEM((feats, levs * half * cols), BF16)
    vm = pl.BlockSpec(memory_space=pltpu.VMEM)
    return pl.pallas_call(
        own_kernel,
        out_shape=(
            n_shape,
            n_shape,
            raw_shape,
            raw_shape,
            VMEM((feats, width), BF16),
            VMEM((half * cols, half * cols), BF16),
            VMEM((2, slots, patches), jnp.int32),
            VMEM((2, slots, patches), F32),
            VMEM((2, slots, patches), F32),
        ),
        in_specs=[pl.BlockSpec(memory_space=pltpu.SMEM)] + [vm] * 6,
        out_specs=[vm] * 9,
        scratch_shapes=[VMEM(n_shape.shape, BF16)],
        compiler_params=PARAMS,
        name="prepare_own",
    )(offs, near(own), near(hw_t), *map(near, obs))


def halo_kernel(offs, halo, n_ref):
    levs, half, _, cols = halo.shape
    rollm = roll_matrix(offs[0], cols)
    for lev in range(levs):
        for r in range(0, half, 2):
            n_ref[:, lev, r * WLON : (r + 2) * WLON, :] = by_window(
                nt(rollm, norm_rows(halo[lev, r])), nt(rollm, norm_rows(halo[lev, r + 1]))
            )


def prepare_halo(offs, halo):
    levs, half, feats, cols = halo.shape
    vm = pl.BlockSpec(memory_space=pltpu.VMEM)
    return pl.pallas_call(
        halo_kernel,
        out_shape=VMEM((cols // WLON, levs, half * WLON, feats), BF16),
        in_specs=[pl.BlockSpec(memory_space=pltpu.SMEM), vm],
        out_specs=vm,
        compiler_params=PARAMS,
    )(offs, near(halo))


def interleave(tasks):
    kinds = [next(task) for task in tasks]
    last = None
    while tasks:
        n = next((i for i, kind in enumerate(kinds) if kind != last), 0)
        task, last = tasks.pop(n), kinds.pop(n)
        kind = next(task, None)
        if kind is not None:
            tasks.append(task)
            kinds.append(kind)


def forecast_kernel(*refs, side, dests, e_loc, heads_loc, ff_loc):
    n_halo, n_own, raw, hw, perm, mine, got, passed = refs[:8]
    outs = refs[8 : 8 + dests]
    (wq, wk, wv, wot, wup, wdt, bias, fscr, theirs) = refs[8 + dests :]
    windows, levs, span, feats = n_own.shape
    half = span // WLON
    n_rows = 2 * half
    wtok = levs * n_rows * WLON
    parts = 2
    cols = windows * WLON
    qtok = levs * half * WLON
    heads = heads_loc * parts
    head_dim = e_loc // heads_loc
    width = hw.shape[1]
    q_row = half - half * side
    band = lax.axis_index("band")
    if side == 0:
        is_open = band > 0
    else:
        is_open = band < lax.axis_size("band") - 1
    penalty = jnp.where(is_open, 0.0, -1000000000.0).astype(F32)

    rows = got.shape[0]
    theirs[pl.ds(pl.multiple_of((band % 2) * rows, 16), rows)] = got[...]
    theirs[pl.ds(pl.multiple_of((1 - band % 2) * rows, 16), rows)] = passed[...]
    w_parts = (mine, theirs)
    n_a = 3 * e_loc * 3 // 2
    n_b = n_a + heads_loc * wtok
    r0 = n_b + e_loc * 3 // 2
    r1 = r0 + ff_loc * 3 // 2
    for p in range(parts):
        qkv = from_dense(w_parts[p][:n_a])
        rows = slice(p * e_loc, (p + 1) * e_loc)
        wq[rows] = qkv[:e_loc]
        wk[rows] = qkv[e_loc : 2 * e_loc]
        wv[rows] = qkv[2 * e_loc :]

    def late_weights():
        yield "M"
        w_out = jnp.concatenate([from_dense(w_parts[p][n_b:r0]) for p in range(parts)], axis=0)
        wot[...] = tn(w_out, eye(heads * head_dim)).astype(BF16)
        for p in range(parts):
            yield "M"
            wup[p * ff_loc : (p + 1) * ff_loc] = from_dense(w_parts[p][r0:r1])
            for i in range(ff_loc // LANES):
                yield "M"
                lo = p * ff_loc + i * LANES
                down = w_parts[p][r1 + i * feats : r1 + (i + 1) * feats].astype(F32) * 0.5
                wdt[:, lo : lo + LANES] = down.astype(BF16)

    lat = (lax.broadcasted_iota(jnp.int32, (wtok, 1), 0) // WLON) % n_rows
    closed = (lat < half) if side == 0 else (lat >= half)
    shut = jnp.where(closed, penalty, 0.0)
    for p in range(parts):
        for h in range(heads_loc):
            rows = []
            for lev in range(levs):
                lo = n_a + h * wtok + lev * n_rows * WLON + q_row * WLON
                rows.append(w_parts[p][lo : lo + span].astype(F32))
            at = (p * heads_loc + h) * LANES
            bias[:, at : at + LANES] = (
                jnp.concatenate(rows * (LANES // qtok), axis=0).T * LOG2E + shut
            )

    first = lax.broadcasted_iota(jnp.int32, (1, LANES), 1) < qtok
    zero = jnp.zeros((), BF16)
    q_scale = head_dim**-0.5 * LOG2E
    e_all = heads * head_dim

    def zeros(rows):
        return jnp.zeros((rows, LANES), BF16)

    s1 = {}

    mixed = {}

    def attention(g, pair, queries):
        yield "M"
        at = slice(g * GROUP + 2 * pair, g * GROUP + 2 * pair + 2)
        order = [n_halo[at], n_own[at]] if side == 0 else [n_own[at], n_halo[at]]
        x_pair = jnp.concatenate(order, axis=2).reshape(2 * wtok, feats)
        k_pair = nt(x_pair, wk[...])
        k0, k1 = k_pair[:wtok], k_pair[wtok:]
        yield "M"
        v_t = nt(wv[...], x_pair).astype(BF16)
        q_t = queries[:, pair * LANES : (pair + 1) * LANES]
        qa = jnp.where(first, q_t, zero)
        qb = jnp.where(first, zero, q_t)
        out = []
        for e0 in range(0, e_all, LANES):
            dims = min(LANES, e_all - e0)
            yield "M"
            lhs = jnp.concatenate([k0[:, e0 : e0 + dims], k1[:, e0 : e0 + dims]], axis=1)
            lhs = lhs.astype(BF16)
            columns = []
            for h in range(dims // head_dim):
                a = e0 + h * head_dim
                gaps = (h * head_dim, dims - (h + 1) * head_dim)
                col = []
                for q in (qa, qb):
                    if gaps[0]:
                        col.append(zeros(gaps[0]))
                    col.append(q[a : a + head_dim])
                    if gaps[1]:
                        col.append(zeros(gaps[1]))
                columns.append(jnp.concatenate(col, axis=0))
            scores = []
            for h in range(0, dims // head_dim, 2):
                yield "M"
                s = nn(lhs, jnp.concatenate(columns[h : h + 2], axis=1))
                scores += [s[:, :LANES], s[:, LANES:]]
            for h in range(0, dims // head_dim, 2):
                probs, inverse = [], []
                for n in (h, h + 1):
                    yield "V"
                    at = (e0 // head_dim + n) * LANES
                    t = scores[n] + bias[:, at : at + LANES]
                    p = jnp.exp2(t - jnp.max(t, axis=0, keepdims=True))
                    inverse.append(1.0 / jnp.sum(p, axis=0, keepdims=True))
                    p = p.astype(BF16)
                    probs.append(
                        jnp.concatenate(
                            [jnp.where(first, p, zero), jnp.where(first, zero, p)], axis=0
                        )
                    )
                yield "M"
                a = e0 + h * head_dim
                o = nn(v_t[a : a + 2 * head_dim], jnp.concatenate(probs, axis=1))
                out.append(o[:head_dim, :LANES] * inverse[0])
                out.append(o[head_dim:, LANES:] * inverse[1])
        mixed[g, pair] = jnp.concatenate(out, axis=0).astype(BF16)

    def project_queries(g):
        x_q = n_own[g * GROUP : (g + 1) * GROUP]
        return (nt(wq[...], x_q.reshape(GROUP * qtok, feats)) * q_scale).astype(BF16)

    def project_out(g):
        at = g * GROUP * qtok
        mix = jnp.concatenate([mixed.pop((g, p)) for p in range(GROUP // 2)], axis=1)
        s1[g] = nn(wot[...], mix) + raw[:, at : at + GROUP * qtok].astype(F32)

    def feed_forward(g):
        yield "V"
        x = s1.pop(g)
        c = x - jnp.mean(x, axis=0, keepdims=True)
        v = jnp.mean(c * c, axis=0, keepdims=True)
        n2 = (c * lax.rsqrt(v + 1e-05)).astype(BF16)
        total = x
        hidden = ff_loc * parts
        acts = []
        for i in range(0, hidden, LANES):
            yield "M"
            up = nn(wup[i : i + LANES], n2)
            yield "V"
            acts.append((up + up * lax.erf(up * math.sqrt(0.5))).astype(BF16))
            if len(acts) == 2 or i + LANES >= hidden:
                yield "M"
                lo = i + LANES - LANES * len(acts)
                total = total + nn(wdt[:, lo : i + LANES], jnp.concatenate(acts, axis=0))
                acts = []
        yield "M"
        f = tn(total.astype(BF16), hw[...])
        for w in range(GROUP):
            at = (g * GROUP + w) * WLON
            fscr[:, :, at : at + WLON, :] = f[w * qtok : (w + 1) * qtok].reshape(
                levs, half, WLON, width
            )

    groups = windows // GROUP
    for g in range(groups + 1):
        tasks = [feed_forward(g - 1)] if g else [late_weights()]
        if g < groups:
            queries = project_queries(g)
            tasks += [attention(g, p, queries) for p in range(GROUP // 2)]
        interleave(tasks)
        if g < groups:
            project_out(g)

    patches = half * (cols // dests)
    for lev in range(levs):
        f = fscr[lev].reshape(half * cols, width).astype(BF16)
        o = tn(f, perm[...]).astype(BF16)
        for d in range(dests):
            outs[d][lev] = o[:, d * patches : (d + 1) * patches]


def forecast(n_halo, n_own, raw, hw, perm, weights, *, side, dests, heads_loc):
    windows, levs, span, feats = n_own.shape
    cols = windows * WLON
    half = span // WLON
    parts = 2
    head_dim = feats // (heads_loc * parts)
    e_loc = heads_loc * head_dim
    width = hw.shape[1]
    wtok = 2 * levs * span
    rows = weights[0].shape[0] - 4 * (e_loc * 3 // 2) - heads_loc * wtok
    ff_loc = rows * 2 * LANES // (3 * LANES + 2 * feats)
    heads = heads_loc * parts
    patches = half * (cols // dests)
    vm = pl.BlockSpec(memory_space=pltpu.VMEM)
    return pl.pallas_call(
        functools.partial(
            forecast_kernel,
            side=side,
            dests=dests,
            e_loc=e_loc,
            heads_loc=heads_loc,
            ff_loc=ff_loc,
        ),
        out_shape=[VMEM((levs, width, patches), BF16)] * dests,
        in_specs=[vm] * 8,
        out_specs=[vm] * dests,
        scratch_shapes=[
            pltpu.VMEM((feats, feats), BF16),
            pltpu.VMEM((feats, feats), BF16),
            pltpu.VMEM((feats, feats), BF16),
            pltpu.VMEM((feats, feats), BF16),
            pltpu.VMEM((ff_loc * parts, feats), BF16),
            pltpu.VMEM((feats, ff_loc * parts), BF16),
            pltpu.VMEM((wtok, heads * LANES), F32),
            pltpu.VMEM((levs, half, cols, width), F32),
            pltpu.VMEM(weights[0].shape, BF16),
        ],
        compiler_params=PARAMS,
    )(*map(near, (n_halo, n_own, raw, hw, perm, *weights)))


def analysis_kernel(*refs, members, side):
    x_refs = refs[:members]
    idx, weight, value = refs[members : members + 3]
    out = refs[-1]
    levs, width, patches = x_refs[0].shape
    slots = idx.shape[1]
    half, cw = out.shape[2], out.shape[3]
    xs = [[x_refs[m][lev].astype(F32) for lev in range(levs)] for m in range(members)]
    state = lax.broadcasted_iota(jnp.int32, (width, patches), 0)
    pairs = [(i, k) for i in range(members) for k in range(i, members)]
    mat = {p: None for p in pairs}
    rhs = [None] * members
    for k in range(slots):
        at = idx[0, k : k + 1]
        hits = [state + lev * width == at for lev in range(levs)]
        y = []
        for m in range(members):
            total = jnp.where(hits[0], xs[m][0], 0.0)
            for lev in range(1, levs):
                total = jnp.where(hits[lev], xs[m][lev], total)
            y.append(jnp.sum(total, axis=0, keepdims=True))
        y_mean = sum(y[1:], y[0]) * (1.0 / members)
        yp = [v - y_mean for v in y]
        r = weight[0, k : k + 1]
        d = value[0, k : k + 1] - y_mean
        for i in range(members):
            ry = r * yp[i]
            for n in range(i, members):
                t = ry * yp[n]
                mat[i, n] = t if k == 0 else mat[i, n] + t
            t = ry * d
            rhs[i] = t if k == 0 else rhs[i] + t
    for i in range(members):
        mat[i, i] = mat[i, i] + (members - 1.0)
    trace = sum([mat[i, i] for i in range(1, members)], mat[0, 0])
    inv = 1.0 / trace

    def entry(a, i, n):
        return a[pairs.index((min(i, n), max(i, n)))]

    def times(a, b):
        res = []
        for i, n in pairs:
            acc = entry(a, i, 0) * entry(b, 0, n)
            for q in range(1, members):
                acc = acc + entry(a, i, q) * entry(b, q, n)
            res.append(acc)
        return res

    def sweep(_, carry):
        g, z = carry
        zg = times(z, g)
        f = [(1.5 if i == n else 0.0) - 0.5 * v for (i, n), v in zip(pairs, zg)]
        return times(g, f), times(f, z)

    g0 = [mat[p] * inv for p in pairs]
    z0 = [jnp.full_like(trace, 1.0 if i == n else 0.0) for i, n in pairs]
    _, z = lax.fori_loop(0, NEWTON, sweep, (g0, z0))
    zz = times(z, z)
    root = math.sqrt(members - 1.0) * lax.rsqrt(trace)
    mean_w = []
    for i in range(members):
        acc = entry(zz, i, 0) * rhs[0]
        for n in range(1, members):
            acc = acc + entry(zz, i, n) * rhs[n]
        mean_w.append(acc * inv)
    me = lax.axis_index("member")
    centers, spreads = [], []
    for lev in range(levs):
        total = xs[0][lev]
        for m in range(1, members):
            total = total + xs[m][lev]
        c = total * (1.0 / members)
        centers.append(c)
        spreads.append([xs[m][lev] - c for m in range(members)])
    for m in range(members):
        w = [mean_w[i] + root * entry(z, i, m) for i in range(members)]
        for lev in range(levs):
            acc = centers[lev]
            for i in range(members):
                acc = acc + spreads[lev][i] * w[i]
            out[m ^ me, lev] = acc.T.reshape(half, cw, width)


def analysis(xs, idx, weight, value, out_shape, side, prev):
    members = len(xs)
    levs, width, patches = xs[0].shape
    _, _, n_rows, cw, _ = out_shape
    half = n_rows // 2
    slots = idx.shape[1]
    vm = pl.BlockSpec(memory_space=pltpu.VMEM)
    obs = pl.BlockSpec((1, slots, patches), lambda i: (side, 0, 0))
    args = [*map(near, (*xs, idx, weight, value))]
    specs = [pl.BlockSpec((levs, width, patches), lambda i: (0, 0, 0))] * members + [obs] * 3
    aliases = {}
    if prev is not None:
        aliases = {len(args): 0}
        args.append(prev)
        specs.append(pl.BlockSpec(memory_space=pl.ANY))
    del vm
    return pl.pallas_call(
        functools.partial(analysis_kernel, members=members, side=side),
        grid=(1,),
        out_shape=jax.ShapeDtypeStruct(out_shape, F32),
        in_specs=specs,
        out_specs=pl.BlockSpec((members, levs, half, cw, width), lambda i: (0, 0, side, 0, 0)),
        input_output_aliases=aliases,
        compiler_params=PARAMS,
    )(*args)


def shards(
    prior_grids,
    w_qkv,
    w_out,
    w_up,
    w_down,
    head_weight,
    pos_bias,
    zonal_offsets,
    obs_index,
    obs_count,
    obs_value,
    obs_weight,
):
    member_grid = prior_grids[0]
    levs = member_grid.shape[0] // lax.axis_size("tensor")
    n_rows = member_grid.shape[1]
    dests = lax.axis_size("member")
    bands = lax.axis_size("band")
    heads_loc = pos_bias.shape[0]

    prior_t = member_grid.swapaxes(2, 3)
    sides = lax.axis_size("tensor")
    mine, piece, own, top, bottom = pack(
        prior_t, w_qkv.transpose(1, 0, 2), w_out, w_up, w_down.T, pos_bias, levs
    )
    got = lax.ppermute(piece, "tensor", [(i, (i + 1) % sides) for i in range(sides)])
    up = [(i, (i + 1) % bands) for i in range(bands)]
    above = lax.ppermute(bottom, "band", up)
    below = lax.ppermute(top, "band", [(b, a) for a, b in up])
    passed = lax.ppermute(got, "band", [(i, i ^ 1) for i in range(bands)])
    obs = (
        obs_index[0].swapaxes(1, 2),
        obs_count[0],
        obs_value[0].swapaxes(1, 2),
        obs_weight[0].swapaxes(1, 2),
    )
    n_own_0, n_own_1, raw_0, raw_1, hw, perm, idx, value, weight = prepare_own(
        zonal_offsets, own, head_weight.T, obs, dests
    )
    n_halo_0 = prepare_halo(zonal_offsets, above)
    n_halo_1 = prepare_halo(zonal_offsets, below)
    cw = obs_index.shape[2]

    received = []
    for side, n_halo, n_own, raw in ((0, n_halo_0, n_own_0, raw_0), (1, n_halo_1, n_own_1, raw_1)):
        if received:
            n_own, _ = lax.optimization_barrier((n_own, received[0][0]))
        sent = forecast(
            n_halo,
            n_own,
            raw,
            hw,
            perm,
            (mine, got, passed),
            side=side,
            dests=dests,
            heads_loc=heads_loc,
        )
        pieces = [sent[0]]
        for k in range(1, dests):
            pieces.append(lax.ppermute(sent[k], "member", [(i, i ^ k) for i in range(dests)]))
        received.append(pieces)
    out_shape = (dests, levs, n_rows, cw, head_weight.shape[1])
    result = None
    for side in range(2):
        result = analysis(received[side], idx, weight, value, out_shape, side, result)
    return result


def solution(mesh):
    return jax.shard_map(
        shards,
        mesh=mesh,
        in_specs=(
            P("member", None, "band", None, None),
            P(None, None, "tensor"),
            P("tensor", None),
            P(None, "tensor"),
            P("tensor", None),
            P(),
            P("tensor", None, None),
            P("member"),
            P("tensor", "band", "member", None),
            P("tensor", "band", "member"),
            P("tensor", "band", "member", None),
            P("tensor", "band", "member", None),
        ),
        out_specs=P(None, "tensor", "band", "member", None),
        check_vma=False,
    )
```
